128 devices in a mesh: slab: 64 (over z, y, x), sub: 2 (over core).
Axes of the slice: x: 4, y: 4, z: 4, core: 2. Of those that a mesh axis runs over, the one named last changes fastest.
Arguments:
- part_cells: int32 [128, 128, 256], P(('slab', 'sub')), may hold values from 0 to 8191
- part_offsets: float32 [128, 128, 3, 256], P(('slab', 'sub')), may hold values from 0 to 1
- part_counts: int32 [128, 128], P(('slab', 'sub')), may hold values from 32 to 256, as said below
- w_first: bfloat16 [16, 27], replicated, may hold values from -1.25 to 1.25
- w_mid: bfloat16 [16, 432], replicated, may hold values from -0.3125 to 0.3125
- w_last: bfloat16 [16, 432], replicated, may hold values from -0.3125 to 0.3125
- w_head: bfloat16 [3, 32], replicated, may hold values from -1 to 1
- cotangent: bfloat16 [3, 256, 16, 256], P(None, 'slab', 'sub'), may hold values from -6 to 6
Outputs:
- force: bfloat16 [3, 256, 16, 256], P(None, 'slab', 'sub')
- grad_first: float32 [16, 27], replicated
- grad_mid: float32 [16, 432], replicated
- grad_last: float32 [16, 432], replicated
- grad_head: float32 [3, 32], replicated
The draws below stay inside these ranges and needn't reach their ends.
Inputs may be any that keep to these rules, and one draw needn't show every extreme that they name: part_counts[s, d] is the number of used slots among the 256 slots from device s to brick d; one brick, drawn from the seed, gets 256 from every device. part_cells[s, d, k] is the cell (i * 8 + j) * 256 + l in brick d's own cells; slots at or above part_counts[s, d] are unused.
All inputs are finite; a program needn't handle non-finite values.
Results may differ from the reference program's by a relative error of at most 0.003.
The reference program's roundings to bfloat16 on the way (of `density_b`, `hidden_one`, `hidden_two`, `hidden_three`, `features`, `grad_three`, `grad_two` and `grad_one`) count: a program that leaves them out, or rounds other values in their place, can miss the bound.
Values may be sent and summed in bfloat16 or wider, within the bound.
A program may use at most 192 MiB of HBM per device.

```python
import math
import jax
import jax.numpy as jnp
from jax import lax

CH = 16
BX = 4
BY = 8
NZ = 256
CAP = 256
NX = 256
NY = 16
NCELLS = 1048576
N_SUB = 2
DEVICES = 128


def draw_part_counts(key, part):
    key_full, key_level, key_drop = jax.random.split(key, 3)
    full_brick = jax.random.randint(key_full, (), 0, DEVICES)
    levels = jax.random.randint(key_level, (DEVICES,), CAP // 4, CAP + 1)
    drops = jax.random.randint(key_drop, (DEVICES, DEVICES), 0, levels[None, :] // 2 + 1)
    counts = levels[None, :] - drops
    column = jnp.arange(DEVICES) == full_brick
    return jnp.where(column[None, :], CAP, counts).astype(jnp.int32)


def place_ends(array, own_key, low, largest):
    spot = [jax.random.randint(jax.random.fold_in(own_key, axis), (), 0, length) for axis, length in enumerate(array.shape)]
    widest = array.shape.index(max(array.shape))
    next_to = spot[:widest] + [(spot[widest] + 1) % array.shape[widest]] + spot[widest + 1:]
    return array.at[tuple(spot)].set(low).at[tuple(next_to)].set(largest)


def block_scale(own_key, dims, shards, least, high):
    gain, own = 1.0, jax.random.fold_in(own_key, 6)
    for axis_at, blocks in shards:
        draws = jnp.exp(jax.random.uniform(jax.random.fold_in(own, axis_at), (blocks,), jnp.float32, least / len(shards), high / len(shards)))
        gain = gain * jnp.repeat(draws, dims[axis_at] // blocks).reshape([-1 if axis == axis_at else 1 for axis in range(len(dims))])
    return gain


def gaussian(own_key, extent, deviation, limit, cuts=(), kind=jnp.bfloat16):
    level = block_scale(own_key, extent, cuts, -0.22, 0.18) if cuts else 1.0
    values = jax.random.normal(own_key, extent, jnp.float32) * deviation * level
    return jnp.minimum(jnp.maximum(values, -limit), limit).astype(kind)


def setup_inputs(seed: int = 0) -> dict:
    streams_of = jax.random.split(jax.random.key(seed), 9)
    return {
        "part_cells": place_ends(jax.random.randint(streams_of[0], (DEVICES, DEVICES, CAP), 0, BX * BY * NZ), jax.random.fold_in(streams_of[0], 1), 0, (BX * BY * NZ) - 1).astype(jnp.int32),
        "part_offsets": jnp.clip(1.0 * jax.random.uniform(streams_of[1], (DEVICES, DEVICES, 3, CAP), jnp.float32) ** block_scale(streams_of[1], (DEVICES, DEVICES, 3, CAP), ((0, 128),), -0.2, 0.2), 0.0, 1.0),
        "part_counts": draw_part_counts(jax.random.fold_in(streams_of[8], 71), 0),
        "w_first": gaussian(streams_of[3], (CH, 27), 27 ** -0.5, 1.25),
        "w_mid": gaussian(streams_of[4], (CH, 27 * CH), (27 * CH) ** -0.5, 0.3125),
        "w_last": gaussian(streams_of[5], (CH, 27 * CH), (27 * CH) ** -0.5, 0.3125),
        "w_head": gaussian(streams_of[6], (3, 2 * CH), (2 * CH) ** -0.5, 1.0),
        "cotangent": gaussian(streams_of[7], (3, NX, NY, NZ), 1.0, 6.0, ((1, 64), (2, 2))),
    }


def wrap_field(field):
    return jnp.pad(field, ((0, 0), (1, 1), (1, 1), (1, 1)), mode='wrap')

def kernel_of(weights, chans):
    out_chans = weights.shape[0]
    return weights.astype(jnp.float32).reshape(out_chans, 3, 3, 3, chans).transpose(0, 4, 1, 2, 3)

def convolve(field, weights):
    chans = field.shape[0]
    padded = wrap_field(field.astype(jnp.float32))
    result = lax.conv_general_dilated(padded[None], kernel_of(weights, chans), (1, 1, 1), 'VALID', dimension_numbers=('NCDHW', 'OIDHW', 'NCDHW'), precision=lax.Precision.HIGHEST)
    return result[0]

def backward(field, weights, grad):
    _, pullback = jax.vjp(convolve, field.astype(jnp.float32), weights.astype(jnp.float32))
    return pullback(grad.astype(jnp.float32))

def silu_slope(value):
    sigma = jax.nn.sigmoid(value)
    return sigma * (1.0 + value * (1.0 - sigma))

def reference(part_cells, part_offsets, part_counts, w_first, w_mid, w_last, w_head, cotangent):
    slot_ids = jnp.arange(CAP, dtype=jnp.int32)
    live = (slot_ids[None, None, :] < part_counts[:, :, None]).astype(jnp.float32)
    bricks = jnp.arange(DEVICES, dtype=jnp.int32)
    base_x = (bricks // N_SUB * BX)[None, :, None]
    base_y = (bricks % N_SUB * BY)[None, :, None]
    cell_x = base_x + part_cells // (BY * NZ)
    cell_y = base_y + part_cells // NZ % BY
    cell_z = part_cells % NZ
    frac_x = part_offsets[:, :, 0, :]
    frac_y = part_offsets[:, :, 1, :]
    frac_z = part_offsets[:, :, 2, :]
    density = jnp.zeros((NX * NY * NZ,), jnp.float32)
    for corner_x in (0, 1):
        weight_x = frac_x if corner_x else 1.0 - frac_x
        for corner_y in (0, 1):
            weight_y = frac_y if corner_y else 1.0 - frac_y
            for corner_z in (0, 1):
                weight_z = frac_z if corner_z else 1.0 - frac_z
                share = live * weight_x * weight_y * weight_z
                index = ((cell_x + corner_x) % NX * NY + (cell_y + corner_y) % NY) * NZ + (cell_z + corner_z) % NZ
                density = density.at[index.reshape(-1)].add(share.reshape(-1))
    density_b = density.reshape(1, NX, NY, NZ).astype(jnp.bfloat16)
    pre_one = convolve(density_b, w_first)
    hidden_one = jax.nn.silu(pre_one).astype(jnp.bfloat16)
    pre_two = convolve(hidden_one, w_mid)
    hidden_two = jax.nn.silu(pre_two).astype(jnp.bfloat16)
    pre_three = convolve(hidden_two, w_last)
    hidden_three = jax.nn.silu(pre_three).astype(jnp.bfloat16)
    features = jnp.concatenate([hidden_three, hidden_one], 0).reshape(2 * CH, -1)
    ct_flat = cotangent.reshape(3, -1)
    force = jnp.dot(w_head, features, preferred_element_type=jnp.float32).astype(jnp.bfloat16).reshape(3, NX, NY, NZ)
    loss_scale = 1.0 / math.sqrt(NCELLS)
    grad_head = loss_scale * jnp.dot(ct_flat, features.T, preferred_element_type=jnp.float32)
    back_features = jnp.dot(w_head.T, ct_flat, preferred_element_type=jnp.float32)
    grad_three = (back_features[:CH] * silu_slope(pre_three.reshape(CH, -1))).astype(jnp.bfloat16).reshape(CH, NX, NY, NZ)
    back_two, grad_last = backward(hidden_two, w_last, grad_three)
    grad_two = (back_two * silu_slope(pre_two)).astype(jnp.bfloat16)
    back_one, grad_mid = backward(hidden_one, w_mid, grad_two)
    back_one = back_one + back_features[CH:].reshape(CH, NX, NY, NZ)
    grad_one = (back_one * silu_slope(pre_one)).astype(jnp.bfloat16)
    _, grad_first = backward(density_b, w_first, grad_one)
    return (force, loss_scale * grad_first, loss_scale * grad_mid, loss_scale * grad_last, grad_head)
```

```python
import functools
import math

import jax
import jax.numpy as jnp
from jax import lax
from jax.experimental import pallas as pl
from jax.experimental.pallas import tpu as pltpu
from jax.sharding import PartitionSpec as P

MESH = pl.DeviceIdType.MESH
F32 = jnp.float32
BF16 = jnp.bfloat16

BX, BY, NZ, CH = 4, 8, 256, 16
COLS = (BX + 2) * CH
CORE = slice(CH, CH + BX * CH)
GROUP = 4
X_ROW = (0, 8, 24, 32, 40)


def lane_roll(value, shift):
    return pltpu.roll(value, shift % value.shape[1], 1)


def dot(a, b):
    return jnp.dot(a, b, preferred_element_type=F32)


def dot_nt(a, b):
    return lax.dot_general(a, b, (((1,), (1,)), ((), ())), preferred_element_type=F32)


def join_z(stacked):
    rows = stacked.shape[0] // 3
    below = lane_roll(stacked[:rows], 1)
    above = lane_roll(stacked[2 * rows :], -1)
    return stacked[rows : 2 * rows] + below + above


def spread_z(grad):
    return jnp.concatenate([lane_roll(grad, -1), grad, lane_roll(grad, 1)], 0).astype(BF16)


def sigmoid(value):
    return 1.0 / (1.0 + jnp.exp(-value))


def slope(value):
    s = sigmoid(value)
    return s * (1.0 + value * (1.0 - s))


def source_terms(tile, half):
    cell = tile.astype(jnp.int32)
    where_z = jnp.where(cell < 0, -1, cell & 255).astype(F32)
    plane = lax.shift_right_arithmetic(cell, 8)

    def spread(value, row, rows=8):
        return jnp.broadcast_to(value[row : row + 1], (rows, 128))

    z_at = spread(where_z, half, NZ).astype(BF16)
    lanes_z = lax.broadcasted_iota(jnp.int32, (NZ, 128), 0).astype(F32).astype(BF16)
    hot = jnp.where(lanes_z == z_at, jnp.ones((), BF16), jnp.zeros((), BF16))
    at = spread(plane, half)
    at_x = lax.shift_right_arithmetic(at, 3)
    at_y = at & 7
    f = spread(tile, 2 + half)
    g = spread(tile, 4 + half)
    h = spread(tile, 6 + half)
    row = lax.broadcasted_iota(jnp.int32, (8, 128), 0)
    zero = jnp.zeros((8, 128), F32)
    weight_y = jnp.where(row == at_y, 1.0 - g, jnp.where(row == at_y + 1, g, zero))
    last_y = jnp.where(at_y == BY - 1, g, zero)
    weight_x = jnp.where(row == at_x, 1.0 - f, jnp.where(row == at_x + 1, f, zero))
    planes = []
    for i in range(BX + 1):
        here = jnp.where(at_x == i, 1.0 - f, jnp.where(at_x == i - 1, f, zero))
        planes.append(here * weight_y)
    planes.insert(2, weight_x * last_y)
    both = jnp.concatenate(planes, 0)
    tall = jnp.broadcast_to(h[:1], (48, 128))
    upper = both * tall
    lower = both - upper
    joint = jnp.concatenate([lower, upper], 0)
    high = joint.astype(BF16)
    low = (joint - high.astype(F32)).astype(BF16)
    return hot, jnp.concatenate([high, low], 0)


def body(
    got, ct, w_one, w_mid, w_last, w_mid_t, w_last_t, w_head, w_head_t,
    force, pay,
    hot_s, wt_s, dep, dep_in, dens_f, dens, one, two, g_three, g_two, pre_one, pre_two, acc,
    send, recv, send_d, recv_d,
):
    n_slab, n_sub = lax.axis_size("slab"), lax.axis_size("sub")
    slab, sub = lax.axis_index("slab"), lax.axis_index("sub")
    up, down, other = (slab + 1) % n_slab, (slab + n_slab - 1) % n_slab, (sub + 1) % n_sub
    neighbours = ((up, sub), (down, sub), (slab, other), (up, other), (down, other))
    barrier = pltpu.get_barrier_semaphore()
    for device in neighbours:
        pl.semaphore_signal(barrier, inc=1, device_id=device, device_id_type=MESH)

    dep2 = jnp.zeros((96, NZ), F32)
    sources = got.shape[0]

    def gather(step, total):
        for part in range(2):
            for k in range(GROUP):
                tile = got[step * 2 * GROUP + part * GROUP + k]
                for half in range(2):
                    hot, weights = source_terms(tile, half)
                    at = k * 256 + half * 128
                    hot_s[part, :, at : at + 128] = hot
                    wt_s[part, :, at : at + 128] = weights
            result = dot_nt(wt_s[part], hot_s[part])
            total = total + result[:96] + result[96:]
        return total

    dep2 = lax.fori_loop(0, sources // (2 * GROUP), gather, dep2)
    dep[...] = dep2[:48] + lane_roll(dep2[48:], 1)

    pl.semaphore_wait(barrier, len(neighbours))

    def remote(src, dst, at, device, sends, recvs):
        return pltpu.make_async_remote_copy(
            src_ref=src, dst_ref=dst, send_sem=sends.at[at], recv_sem=recvs.at[at],
            device_id=device, device_id_type=MESH,
        )

    upper_rows, lower_rows = pl.ds(16, 32), pl.ds(0, 24)
    copies = []
    for at, (device, rows) in enumerate(
        zip(neighbours, (upper_rows, lower_rows, pl.ds(0, 48), upper_rows, lower_rows))
    ):
        copies.append(remote(dep.at[rows], dep_in.at[at, rows], at, device, send_d, recv_d))
    for copy in copies:
        copy.start()

    dens_f[...] = jnp.zeros_like(dens_f)

    def place(source, source_x, x):
        base = (x + 2) * 16
        dens_f[base + 2 : base + 10] += source[X_ROW[source_x] : X_ROW[source_x] + 8]
        dens_f[base + 10 : base + 11] += source[16 + source_x : 17 + source_x]

    def place_other(source, source_x, x):
        base, row = (x + 2) * 16, X_ROW[source_x]
        dens_f[base : base + 2] += source[row + 6 : row + 8]
        dens_f[base + 2 : base + 3] += source[16 + source_x : 17 + source_x]
        dens_f[base + 10 : base + 12] += source[row : row + 2]

    for x in range(BX + 1):
        place(dep, x, x)
    for copy in copies:
        copy.wait()
    for x in (2, 3, 4):
        place(dep_in.at[0], x, x - 4)
    for x in (0, 1):
        place(dep_in.at[1], x, x + 4)
    for x in range(BX + 1):
        place_other(dep_in.at[2], x, x)
    for x in (2, 3, 4):
        place_other(dep_in.at[3], x, x - 4)
    for x in (0, 1):
        place_other(dep_in.at[4], x, x + 4)
    dens[...] = dens_f[...].astype(BF16)

    for y in range(BY + 2):
        taps = lane_roll(w_one[...], y).astype(BF16)
        pre = join_z(dot(taps, dens[...]))
        one[y] = (pre * sigmoid(pre)).astype(BF16)
        if 1 <= y <= BY:
            pre_one[y - 1] = pre[CORE]

    def rims(field, base):
        right, left = pl.ds(BX * CH, CH), pl.ds(CH, CH)
        before, after = pl.ds(0, CH), pl.ds((BX + 1) * CH, CH)
        core, ys = pl.ds(CH, BX * CH), pl.ds(1, BY)
        plan = (
            ((up, sub), (ys, right), (ys, before)),
            ((down, sub), (ys, left), (ys, after)),
            ((slab, other), (1, core), (BY + 1, core)),
            ((slab, other), (BY, core), (0, core)),
            ((up, other), (1, right), (BY + 1, before)),
            ((up, other), (BY, right), (0, before)),
            ((down, other), (1, left), (BY + 1, after)),
            ((down, other), (BY, left), (0, after)),
        )
        started = []
        for at, (device, src, dst) in enumerate(plan):
            copy = remote(field.at[src], field.at[dst], base + at, device, send, recv)
            copy.start()
            started.append(copy)
        return started

    def planes(field, y):
        return field[y : y + 3].reshape(3 * COLS, NZ)

    def conv(taps, field, y):
        return join_z(dot(taps[...], planes(field, y)))

    for y in range(BY):
        pre = conv(w_mid, one, y)
        pre_two[y] = pre
        two[y + 1, CORE] = (pre * sigmoid(pre)).astype(BF16)
    for copy in rims(two, 0):
        copy.wait()

    heads = []
    for y in range(BY):
        pre = conv(w_last, two, y)
        s = sigmoid(pre)
        features = jnp.concatenate([(pre * s).astype(BF16), one[y + 1, CORE]], 0)
        force[y] = dot(w_head[...], features).astype(BF16)
        heads.append((ct[y], features))
        back = dot(w_head_t[: BX * CH], ct[y])
        g_three[y + 1, CORE] = (back * (s * (1.0 + pre * (1.0 - s)))).astype(BF16)
    started = rims(g_three, 8)
    head = dot_nt(*heads[0])
    for pair in heads[1:]:
        head = head + dot_nt(*pair)

    def weight_grad(grads, field, shift):
        acc[:, 3 * COLS :] = jnp.zeros((192, 96), F32)
        for y in range(BY):
            term = dot_nt(spread_z(grads[y + 1, CORE].astype(F32)), planes(field, y))
            if y == 0:
                acc[:, : 3 * COLS] = term
            else:
                acc[:, : 3 * COLS] += term
        rows = []
        for dz in range(3):
            total = jnp.zeros((CH, 384), F32)
            for x in range(BX):
                at = (dz * BX + x) * CH
                total = total + lane_roll(acc[at : at + CH], -CH * x)
            rows.append(total)
        joint = jnp.concatenate(rows, 0)
        lane = lax.broadcasted_iota(jnp.int32, joint.shape, 1)
        joint = jnp.where((lane % 96 < 48) & (lane < 3 * COLS), joint, 0.0)
        return lane_roll(joint, shift) if shift else joint

    sums = weight_grad(g_three, two, 48)
    for copy in started:
        copy.wait()

    for y in range(BY):
        back = conv(w_last_t, g_three, y)
        g_two[y + 1, CORE] = (back * slope(pre_two[y])).astype(BF16)
    started = rims(g_two, 16)
    sums = sums + weight_grad(g_two, one, 0)
    for copy in started:
        copy.wait()

    first = jnp.zeros((192, 128), F32)
    for y in range(BY):
        back = conv(w_mid_t, g_two, y) + dot(w_head_t[BX * CH :], ct[y])
        grad = (back * slope(pre_one[y])).astype(BF16).astype(F32)
        first = first + lane_roll(dot_nt(spread_z(grad), dens[...]), -y)
    rows = []
    for dz in range(3):
        total = jnp.zeros((CH, 128), F32)
        for x in range(BX):
            at = (dz * BX + x) * CH
            total = total + lane_roll(first[at : at + CH], -(16 * x + 17))
        rows.append(total)
    joint = jnp.concatenate(rows, 0)
    lane = lax.broadcasted_iota(jnp.int32, joint.shape, 1)
    joint = jnp.where((lane % 16 < 3) & (lane < 48), joint, 0.0)
    extra = lane_roll(joint, 32)
    lane = lax.broadcasted_iota(jnp.int32, (16, 128), 1)
    row = lax.broadcasted_iota(jnp.int32, (16, 128), 0)
    total = jnp.zeros((16, 128), F32)
    for x in range(BX):
        mine = (row % BX == x) & (lane % 64 < CH)
        total = total + jnp.where(mine, lane_roll(head, -CH * x), 0.0)
    total = jnp.where(lane < CH, total, 0.0) + jnp.where(
        (lane >= CH) & (lane < 2 * CH), lane_roll(total, -48), 0.0
    )
    total = lane_roll(total, 80)
    pay[...] = sums
    pay[:, 256:384] += extra
    pay[:16, 256:384] += total


def wide_taps(weights):
    shaped = weights.reshape(CH, 3, 3, 3, CH).transpose(3, 0, 2, 1, 4)
    rows = [jnp.pad(shaped, ((0, 0), (0, 0), (0, 0), (x, BX - 1 - x), (0, 0))) for x in range(BX)]
    return jnp.stack(rows, 1).reshape(3 * BX * CH, 3 * COLS)


def flipped(weights):
    shaped = weights.reshape(CH, 3, 3, 3, CH)[:, ::-1, ::-1, ::-1]
    return shaped.transpose(4, 1, 2, 3, 0).reshape(CH, 27 * CH)


def first_taps(weights):
    width = BX + 2
    shaped = weights.reshape(CH, 3, 3, 3).transpose(3, 0, 1, 2)
    rows = [
        jnp.pad(shaped, ((0, 0), (0, 0), (x, width - 1 - x), (0, 13))) for x in range(width)
    ]
    return jnp.stack(rows, 1).reshape(3 * width * CH, 128).astype(F32)


def head_taps(weights):
    halves = weights.reshape(3, 1, 2, 1, CH) * jnp.eye(BX, dtype=BF16).reshape(1, BX, 1, BX, 1)
    return jnp.pad(halves.reshape(3 * BX, 2 * BX * CH), ((0, 4), (0, 0)))


def per_device(part_cells, part_offsets, part_counts, w_first, w_mid, w_last, w_head, cotangent):
    n_slab, n_sub = lax.axis_size("slab"), lax.axis_size("sub")
    devices = n_slab * n_sub
    slots = part_cells.shape[2]
    live = jnp.arange(slots, dtype=jnp.int32)[None, :] < part_counts[0][:, None]
    cells = jnp.where(live, part_cells[0], -1).astype(F32).reshape(devices, 2, 128)
    packed = jnp.concatenate([cells, part_offsets[0].reshape(devices, 6, 128)], 1)
    got = lax.all_to_all(packed, ("slab", "sub"), split_axis=0, concat_axis=0, tiled=True)
    ct = cotangent.transpose(2, 0, 1, 3).reshape(BY, 3 * BX, NZ)
    ct = jnp.pad(ct, ((0, 0), (0, 4), (0, 0)))
    head = head_taps(w_head)
    vmem = pl.BlockSpec(memory_space=pltpu.VMEM)
    field = pltpu.VMEM((BY + 2, COLS, NZ), BF16)
    kept = pltpu.VMEM((BY, BX * CH, NZ), F32)
    force, pay = pl.pallas_call(
        body,
        out_shape=(
            jax.ShapeDtypeStruct((BY, 16, NZ), BF16),
            jax.ShapeDtypeStruct((48, 384), F32),
        ),
        in_specs=[vmem] * 9,
        out_specs=(vmem, vmem),
        scratch_shapes=[
            pltpu.VMEM((2, NZ, 256 * GROUP), BF16),
            pltpu.VMEM((2, 192, 256 * GROUP), BF16),
            pltpu.VMEM((48, NZ), F32),
            pltpu.VMEM((5, 48, NZ), F32),
            pltpu.VMEM((128, NZ), F32),
            pltpu.VMEM((128, NZ), BF16),
            field, field, field, field, kept, kept,
            pltpu.VMEM((192, 384), F32),
            pltpu.SemaphoreType.DMA((24,)),
            pltpu.SemaphoreType.DMA((24,)),
            pltpu.SemaphoreType.DMA((5,)),
            pltpu.SemaphoreType.DMA((5,)),
        ],
        compiler_params=pltpu.CompilerParams(
            collective_id=0, has_side_effects=True, vmem_limit_bytes=48 << 20
        ),
        name="level",
    )(
        got, ct, first_taps(w_first), wide_taps(w_mid), wide_taps(w_last),
        wide_taps(flipped(w_mid)), wide_taps(flipped(w_last)), head, head.T,
    )
    loss_scale = 1.0 / math.sqrt(BX * n_slab * BY * n_sub * NZ)
    pay = loss_scale * lax.psum(pay, ("slab", "sub"))
    both = pay[:, :288].reshape(3, CH, 3, 2, 3, CH).transpose(3, 1, 4, 2, 0, 5)
    both = both.reshape(2, CH, 27 * CH)
    first = pay[:, 288:336].reshape(3, CH, 3, 16)[..., :3].transpose(1, 2, 3, 0)
    top = pay[:12, 336:368].reshape(3, BX, 2 * CH).sum(1)
    force = force[:, : 3 * BX].reshape(BY, 3, BX, NZ).transpose(1, 2, 0, 3)
    return force, first.reshape(CH, 27), both[0], both[1], top


def solution(mesh):
    in_specs = (
        P(("slab", "sub"), None, None),
        P(("slab", "sub"), None, None, None),
        P(("slab", "sub"), None),
        P(), P(), P(), P(),
        P(None, "slab", "sub", None),
    )
    out_specs = (P(None, "slab", "sub", None), P(), P(), P(), P())
    return jax.shard_map(
        per_device, mesh=mesh, in_specs=in_specs, out_specs=out_specs, check_vma=False
    )
```

```python
import functools
import math

import jax
import jax.numpy as jnp
from jax import lax
from jax.experimental import pallas as pl
from jax.experimental.pallas import tpu as pltpu
from jax.sharding import PartitionSpec as P

MESH = pl.DeviceIdType.MESH
F32 = jnp.float32
BF16 = jnp.bfloat16

BX, BY, NZ, CH = 4, 8, 256, 16
COLS = (BX + 2) * CH
CORE = slice(CH, CH + BX * CH)
GROUP = 4
X_ROW = (0, 8, 24, 32, 40)


def lane_roll(value, shift):
    return pltpu.roll(value, shift % value.shape[1], 1)


def dot(a, b):
    return jnp.dot(a, b, preferred_element_type=F32)


def dot_nt(a, b):
    return lax.dot_general(a, b, (((1,), (1,)), ((), ())), preferred_element_type=F32)


def join_z(stacked):
    rows = stacked.shape[0] // 3
    below = lane_roll(stacked[:rows], 1)
    above = lane_roll(stacked[2 * rows :], -1)
    return stacked[rows : 2 * rows] + below + above


def spread_z(grad):
    return jnp.concatenate([lane_roll(grad, -1), grad, lane_roll(grad, 1)], 0).astype(BF16)


def sigmoid(value):
    return 1.0 / (1.0 + jnp.exp(-value))


def slope(value):
    s = sigmoid(value)
    return s * (1.0 + value * (1.0 - s))


def source_terms(tile, half):
    cell = tile.astype(jnp.int32)
    where_z = jnp.where(cell < 0, -1, cell & 255).astype(F32)
    plane = lax.shift_right_arithmetic(cell, 8)

    def spread(value, row, rows=8):
        return jnp.broadcast_to(value[row : row + 1], (rows, 128))

    z_at = spread(where_z, half, NZ).astype(BF16)
    lanes_z = lax.broadcasted_iota(jnp.int32, (NZ, 128), 0).astype(F32).astype(BF16)
    hot = jnp.where(lanes_z == z_at, jnp.ones((), BF16), jnp.zeros((), BF16))
    at = spread(plane, half)
    at_x = lax.shift_right_arithmetic(at, 3)
    at_y = at & 7
    f = spread(tile, 2 + half)
    g = spread(tile, 4 + half)
    h = spread(tile, 6 + half)
    row = lax.broadcasted_iota(jnp.int32, (8, 128), 0)
    zero = jnp.zeros((8, 128), F32)
    weight_y = jnp.where(row == at_y, 1.0 - g, jnp.where(row == at_y + 1, g, zero))
    last_y = jnp.where(at_y == BY - 1, g, zero)
    weight_x = jnp.where(row == at_x, 1.0 - f, jnp.where(row == at_x + 1, f, zero))
    planes = []
    for i in range(BX + 1):
        here = jnp.where(at_x == i, 1.0 - f, jnp.where(at_x == i - 1, f, zero))
        planes.append(here * weight_y)
    planes.insert(2, weight_x * last_y)
    both = jnp.concatenate(planes, 0)
    tall = jnp.broadcast_to(h[:1], (48, 128))
    upper = both * tall
    lower = both - upper
    joint = jnp.concatenate([lower, upper], 0)
    high = joint.astype(BF16)
    low = (joint - high.astype(F32)).astype(BF16)
    return hot, jnp.concatenate([high, low], 0)


def body(
    got, ct, w_first, w_mid_in, w_last_in, w_head_in,
    force, grad_first, grad_mid, grad_last, grad_head,
    hot_s, wt_s, dep, dep_in, dens_f, dens, one, two, g_three, g_two, pre_one, pre_two, acc,
    base, w_one, w_mid, w_last, w_mid_t, w_last_t, head_f, head_b, ct_s, pay, half_in, ring, whole,
    send, recv, send_d, recv_d, send_s, recv_s,
):
    n_slab, n_sub = lax.axis_size("slab"), lax.axis_size("sub")
    slab, sub = lax.axis_index("slab"), lax.axis_index("sub")
    up, down, other = (slab + 1) % n_slab, (slab + n_slab - 1) % n_slab, (sub + 1) % n_sub
    neighbours = ((up, sub), (down, sub), (slab, other), (up, other), (down, other))
    axes = []
    for stride in (1, 4, 16):
        size = min(4, max(1, n_slab // stride))
        at = slab // stride % size
        axes.append((at, [slab + ((at + i) % size - at) * stride for i in range(1, size)]))
    partners = [(peer, sub) for _, peers in axes for peer in peers]
    barrier = pltpu.get_barrier_semaphore()
    for device in (*neighbours, *partners):
        pl.semaphore_signal(barrier, inc=1, device_id=device, device_id_type=MESH)

    make_tables(w_first, w_mid_in, w_last_in, w_head_in, base, w_one, w_mid, w_last, w_mid_t,
                w_last_t, head_f, head_b)
    ct_s[...] = jnp.zeros_like(ct_s)
    for k in range(3):
        for x in range(BX):
            at = (k * BX + x) * BY
            ct_s[at : at + BY] = ct[k, x]

    dep2 = jnp.zeros((96, NZ), F32)
    sources = got.shape[0]

    def gather(step, total):
        for part in range(2):
            for k in range(GROUP):
                tile = got[step * 2 * GROUP + part * GROUP + k]
                for half in range(2):
                    hot, weights = source_terms(tile, half)
                    at = k * 256 + half * 128
                    hot_s[part, :, at : at + 128] = hot
                    wt_s[part, :, at : at + 128] = weights
            result = dot_nt(wt_s[part], hot_s[part])
            total = total + result[:96] + result[96:]
        return total

    dep2 = lax.fori_loop(0, sources // (2 * GROUP), gather, dep2)
    dep[...] = dep2[:48] + lane_roll(dep2[48:], 1)

    pl.semaphore_wait(barrier, len(neighbours) + len(partners))

    def remote(src, dst, at, device, sends, recvs):
        return pltpu.make_async_remote_copy(
            src_ref=src, dst_ref=dst, send_sem=sends.at[at], recv_sem=recvs.at[at],
            device_id=device, device_id_type=MESH,
        )

    upper_rows, lower_rows = pl.ds(16, 32), pl.ds(0, 24)
    copies = []
    for at, (device, rows) in enumerate(
        zip(neighbours, (upper_rows, lower_rows, pl.ds(0, 48), upper_rows, lower_rows))
    ):
        copies.append(remote(dep.at[rows], dep_in.at[at, rows], at, device, send_d, recv_d))
    for copy in copies:
        copy.start()

    dens_f[...] = jnp.zeros_like(dens_f)

    def place(source, source_x, x):
        base = (x + 2) * 16
        dens_f[base + 2 : base + 10] += source[X_ROW[source_x] : X_ROW[source_x] + 8]
        dens_f[base + 10 : base + 11] += source[16 + source_x : 17 + source_x]

    def place_other(source, source_x, x):
        base, row = (x + 2) * 16, X_ROW[source_x]
        dens_f[base : base + 2] += source[row + 6 : row + 8]
        dens_f[base + 2 : base + 3] += source[16 + source_x : 17 + source_x]
        dens_f[base + 10 : base + 12] += source[row : row + 2]

    for x in range(BX + 1):
        place(dep, x, x)
    for copy in copies:
        copy.wait()
    for x in (2, 3, 4):
        place(dep_in.at[0], x, x - 4)
    for x in (0, 1):
        place(dep_in.at[1], x, x + 4)
    for x in range(BX + 1):
        place_other(dep_in.at[2], x, x)
    for x in (2, 3, 4):
        place_other(dep_in.at[3], x, x - 4)
    for x in (0, 1):
        place_other(dep_in.at[4], x, x + 4)
    dens[...] = dens_f[...].astype(BF16)

    for y in range(BY + 2):
        taps = lane_roll(w_one[...], y).astype(BF16)
        pre = join_z(dot(taps, dens[...]))
        one[y] = (pre * sigmoid(pre)).astype(BF16)
        if 1 <= y <= BY:
            pre_one[y - 1] = pre[CORE]

    def rims(field, base):
        right, left = pl.ds(BX * CH, CH), pl.ds(CH, CH)
        before, after = pl.ds(0, CH), pl.ds((BX + 1) * CH, CH)
        core, ys = pl.ds(CH, BX * CH), pl.ds(1, BY)
        plan = (
            ((up, sub), (ys, right), (ys, before)),
            ((down, sub), (ys, left), (ys, after)),
            ((slab, other), (1, core), (BY + 1, core)),
            ((slab, other), (BY, core), (0, core)),
            ((up, other), (1, right), (BY + 1, before)),
            ((up, other), (BY, right), (0, before)),
            ((down, other), (1, left), (BY + 1, after)),
            ((down, other), (BY, left), (0, after)),
        )
        started = []
        for at, (device, src, dst) in enumerate(plan):
            copy = remote(field.at[src], field.at[dst], base + at, device, send, recv)
            copy.start()
            started.append(copy)
        return started

    def planes(field, y):
        return field[y : y + 3].reshape(3 * COLS, NZ)

    def conv(taps, field, y):
        return join_z(dot(taps[...], planes(field, y)))

    for y in range(BY):
        pre = conv(w_mid, one, y)
        pre_two[y] = pre
        two[y + 1, CORE] = (pre * sigmoid(pre)).astype(BF16)
    for copy in rims(two, 0):
        copy.wait()

    row_y = lax.broadcasted_iota(jnp.int32, (128, 128), 0) % BY
    lane_y = lax.broadcasted_iota(jnp.int32, (128, 128), 1) % BY
    out = jnp.zeros((96, NZ), F32)
    head = jnp.zeros((128, 128), F32)
    for y in range(BY):
        pre = conv(w_last, two, y)
        s = sigmoid(pre)
        features = jnp.concatenate([(pre * s).astype(BF16), one[y + 1, CORE]], 0)
        taps = jnp.where(row_y == y, head_f[...], 0.0)[:96].astype(BF16)
        out = out + dot(taps, features)
        head = head + jnp.where(row_y == y, dot_nt(ct_s[...], features), 0.0)
        taps = jnp.where(lane_y == y, head_b[...], 0.0)[: BX * CH].astype(BF16)
        back = dot(taps, ct_s[...])
        g_three[y + 1, CORE] = (back * (s * (1.0 + pre * (1.0 - s)))).astype(BF16)
    started = rims(g_three, 8)
    for k in range(3):
        for x in range(BX):
            at = (k * BX + x) * BY
            force[k, x] = out[at : at + BY].astype(BF16)

    def weight_grad(grads, field, shift):
        acc[:, 3 * COLS :] = jnp.zeros((192, 96), F32)
        for y in range(BY):
            term = dot_nt(spread_z(grads[y + 1, CORE].astype(F32)), planes(field, y))
            if y == 0:
                acc[:, : 3 * COLS] = term
            else:
                acc[:, : 3 * COLS] += term
        rows = []
        for dz in range(3):
            total = jnp.zeros((CH, 384), F32)
            for x in range(BX):
                at = (dz * BX + x) * CH
                total = total + lane_roll(acc[at : at + CH], -CH * x)
            rows.append(total)
        joint = jnp.concatenate(rows, 0)
        lane = lax.broadcasted_iota(jnp.int32, joint.shape, 1)
        joint = jnp.where((lane % 96 < 48) & (lane < 3 * COLS), joint, 0.0)
        return lane_roll(joint, shift) if shift else joint

    sums = weight_grad(g_three, two, 48)
    for copy in started:
        copy.wait()

    for y in range(BY):
        back = conv(w_last_t, g_three, y)
        g_two[y + 1, CORE] = (back * slope(pre_two[y])).astype(BF16)
    started = rims(g_two, 16)
    sums = sums + weight_grad(g_two, one, 0)
    for copy in started:
        copy.wait()

    first = jnp.zeros((192, 128), F32)
    for y in range(BY):
        taps = jnp.where(lane_y == y, head_b[...], 0.0)[BX * CH :].astype(BF16)
        back = conv(w_mid_t, g_two, y) + dot(taps, ct_s[...])
        grad = (back * slope(pre_one[y])).astype(BF16).astype(F32)
        first = first + lane_roll(dot_nt(spread_z(grad), dens[...]), -y)
    rows = []
    for dz in range(3):
        total = jnp.zeros((CH, 128), F32)
        for x in range(BX):
            at = (dz * BX + x) * CH
            total = total + lane_roll(first[at : at + CH], -(16 * x + 17))
        rows.append(total)
    joint = jnp.concatenate(rows, 0)
    lane = lax.broadcasted_iota(jnp.int32, joint.shape, 1)
    joint = jnp.where((lane % 16 < 3) & (lane < 48), joint, 0.0)
    extra = lane_roll(joint, 32)
    row = lax.broadcasted_iota(jnp.int32, (128, 128), 0)
    lane = lax.broadcasted_iota(jnp.int32, (128, 128), 1)
    head = jnp.where(lane % 64 // CH == row // BY % BX, head, 0.0)
    kept = jnp.concatenate(
        [jnp.sum(head[k * 32 : k * 32 + 32], 0, keepdims=True) for k in range(3)]
        + [jnp.zeros((5, 128), F32)],
        0,
    )
    kept = kept + lane_roll(kept, -2 * CH)
    kept = kept + lane_roll(kept, -CH)
    lane = lax.broadcasted_iota(jnp.int32, (8, 128), 1)
    top = jnp.where(lane < CH, kept, 0.0) + jnp.where(
        (lane >= CH) & (lane < 2 * CH), lane_roll(kept, -48), 0.0
    )
    top = lane_roll(top, 80)
    pay[...] = sums
    pay[:, 256:384] += extra
    pay[:8, 256:384] += top

    theirs = pl.ds(pl.multiple_of(other * 24, 8), 24)
    mine = pl.ds(pl.multiple_of(sub * 24, 8), 24)
    copy = remote(pay.at[theirs], half_in, 0, (slab, other), send_s, recv_s)
    copy.start()
    copy.wait()
    total = pay[mine] + half_in[...]
    at_sem = 1
    for turn in range(3):
        copies = []
        for part in range(3):
            at, peers = axes[(part + turn) % 3]
            rows = pl.ds(part * 8, 8)
            ring[turn, at, rows] = total[part * 8 : part * 8 + 8]
            for peer in peers:
                slot = ring.at[turn, at, rows]
                copies.append(remote(slot, slot, at_sem, (peer, sub), send_s, recv_s))
                copies[-1].start()
                at_sem += 1
        for copy in copies:
            copy.wait()
        parts = []
        for part in range(3):
            size = len(axes[(part + turn) % 3][1]) + 1
            rows = slice(part * 8, part * 8 + 8)
            value = ring[turn, 0, rows]
            for slot in range(1, size):
                value = value + ring[turn, slot, rows]
            parts.append(value)
        total = jnp.concatenate(parts, 0)
    whole[mine] = total * (1.0 / math.sqrt(BX * n_slab * BY * n_sub * NZ))
    copy = remote(whole.at[mine], whole.at[mine], at_sem, (slab, other), send_s, recv_s)
    copy.start()
    copy.wait()
    for dx, dy, dz in OFFSETS:
        rows, tap = slice(dz * CH, dz * CH + CH), dx * 9 + dy * 3 + dz
        at, to = dy * 96 + dx * CH, slice(tap * CH, tap * CH + CH)
        grad_mid[:, to] = whole[rows, at : at + CH]
        grad_last[:, to] = whole[rows, at + 48 : at + 48 + CH]
        at = 288 + dx * CH + dy
        grad_first[:, tap : tap + 1] = whole[rows, at : at + 1]
    grad_head[...] = whole[:3, 336:368]


OFFSETS = [(dx, dy, dz) for dx in range(3) for dy in range(3) for dz in range(3)]


def make_tables(w_first, w_mid, w_last, w_head, base, one, mid, last, mid_t, last_t, head_f, head_b):
    def spread(out):
        for dz in range(3):
            for x in range(BX):
                at = (dz * BX + x) * CH
                moved = lane_roll(base[dz * CH : dz * CH + CH], x * CH)
                out[at : at + CH] = moved[:, : 3 * COLS].astype(BF16)

    base[...] = jnp.zeros_like(base)
    for source, out, out_t in ((w_mid, mid, mid_t), (w_last, last, last_t)):
        weights = source[...].astype(F32)
        for dx, dy, dz in OFFSETS:
            tap, at = dx * 9 + dy * 3 + dz, dy * 96 + dx * CH
            base[dz * CH : dz * CH + CH, at : at + CH] = weights[:, tap * CH : tap * CH + CH]
        spread(out)
        padded = jnp.concatenate([weights, jnp.zeros((CH, 80), F32)], 1)
        turned = jnp.concatenate([padded, jnp.zeros((112, 512), F32)], 0).T
        for dx, dy, dz in OFFSETS:
            tap, at = dx * 9 + dy * 3 + dz, (2 - dy) * 96 + (2 - dx) * CH
            to = (2 - dz) * CH
            base[to : to + CH, at : at + CH] = turned[tap * CH : tap * CH + CH, :CH]
        spread(out_t)
    base[...] = jnp.zeros_like(base)
    weights = w_first[...].astype(F32)
    for dx, dy, dz in OFFSETS:
        tap, at = dx * 9 + dy * 3 + dz, dx * 16 + dy
        base[dz * CH : dz * CH + CH, at : at + 1] = weights[:, tap : tap + 1]
    for dz in range(3):
        for x in range(BX + 2):
            at = (dz * (BX + 2) + x) * CH
            one[at : at + CH] = lane_roll(base[dz * CH : dz * CH + CH, :128], x * 16)
    head_f[...] = jnp.zeros_like(head_f)
    weights = w_head[...].astype(F32)
    for k in range(3):
        for x in range(BX):
            at = (k * BX + x) * BY
            for half in range(2):
                row = weights[k : k + 1, half * CH : half * CH + CH]
                to = half * 64 + x * CH
                head_f[at : at + BY, to : to + CH] = jnp.broadcast_to(row, (BY, CH))
    head_b[...] = head_f[...].T


def per_device(part_cells, part_offsets, part_counts, w_first, w_mid, w_last, w_head, cotangent):
    n_slab, n_sub = lax.axis_size("slab"), lax.axis_size("sub")
    devices = n_slab * n_sub
    slots = part_cells.shape[2]
    live = jnp.arange(slots, dtype=jnp.int32)[None, :] < part_counts[0][:, None]
    cells = jnp.where(live, part_cells[0], -1).astype(F32).reshape(devices, 2, 128)
    packed = jnp.concatenate([cells, part_offsets[0].reshape(devices, 6, 128)], 1)
    got = lax.all_to_all(packed, ("slab", "sub"), split_axis=0, concat_axis=0, tiled=True)
    vmem = pl.BlockSpec(memory_space=pltpu.VMEM)
    field = pltpu.VMEM((BY + 2, COLS, NZ), BF16)
    kept = pltpu.VMEM((BY, BX * CH, NZ), F32)
    table = pltpu.VMEM((192, 3 * COLS), BF16)
    return pl.pallas_call(
        body,
        out_shape=(
            jax.ShapeDtypeStruct(cotangent.shape, BF16),
            jax.ShapeDtypeStruct(w_first.shape, F32),
            jax.ShapeDtypeStruct(w_mid.shape, F32),
            jax.ShapeDtypeStruct(w_last.shape, F32),
            jax.ShapeDtypeStruct(w_head.shape, F32),
        ),
        in_specs=[vmem] * 6,
        out_specs=[vmem] * 5,
        scratch_shapes=[
            pltpu.VMEM((2, NZ, 256 * GROUP), BF16),
            pltpu.VMEM((2, 192, 256 * GROUP), BF16),
            pltpu.VMEM((48, NZ), F32),
            pltpu.VMEM((5, 48, NZ), F32),
            pltpu.VMEM((128, NZ), F32),
            pltpu.VMEM((128, NZ), BF16),
            field, field, field, field, kept, kept,
            pltpu.VMEM((192, 384), F32),
            pltpu.VMEM((48, 384), F32),
            pltpu.VMEM((288, 128), F32),
            table, table, table, table,
            pltpu.VMEM((128, 128), F32),
            pltpu.VMEM((128, 128), F32),
            pltpu.VMEM((128, NZ), BF16),
            pltpu.VMEM((48, 384), F32),
            pltpu.VMEM((24, 384), F32),
            pltpu.VMEM((3, 4, 24, 384), F32),
            pltpu.VMEM((48, 384), F32),
            pltpu.SemaphoreType.DMA((24,)),
            pltpu.SemaphoreType.DMA((24,)),
            pltpu.SemaphoreType.DMA((5,)),
            pltpu.SemaphoreType.DMA((5,)),
            pltpu.SemaphoreType.DMA((29,)),
            pltpu.SemaphoreType.DMA((29,)),
        ],
        compiler_params=pltpu.CompilerParams(
            collective_id=0, has_side_effects=True, vmem_limit_bytes=48 << 20
        ),
        name="level",
    )(got, cotangent, w_first, w_mid, w_last, w_head)


def solution(mesh):
    in_specs = (
        P(("slab", "sub"), None, None),
        P(("slab", "sub"), None, None, None),
        P(("slab", "sub"), None),
        P(), P(), P(), P(),
        P(None, "slab", "sub", None),
    )
    out_specs = (P(None, "slab", "sub", None), P(), P(), P(), P())
    return jax.shard_map(
        per_device, mesh=mesh, in_specs=in_specs, out_specs=out_specs, check_vma=False
    )
```

```python
import functools
import math

import jax
import jax.numpy as jnp
from jax import lax
from jax.experimental import pallas as pl
from jax.experimental.pallas import tpu as pltpu
from jax.sharding import PartitionSpec as P

MESH = pl.DeviceIdType.MESH
F32 = jnp.float32
BF16 = jnp.bfloat16

BX, BY, NZ, CH = 4, 8, 256, 16
COLS = (BX + 2) * CH
CORE = slice(CH, CH + BX * CH)
GROUP = 4
SPREAD = 1
X_ROW = (0, 8, 24, 32, 40)


def lane_roll(value, shift):
    return pltpu.roll(value, shift % value.shape[1], 1)


def dot(a, b):
    return jnp.dot(a, b, preferred_element_type=F32)


def dot_nt(a, b):
    return lax.dot_general(a, b, (((1,), (1,)), ((), ())), preferred_element_type=F32)


def join_z(stacked):
    rows = stacked.shape[0] // 3
    below = lane_roll(stacked[:rows], 1)
    above = lane_roll(stacked[2 * rows :], -1)
    return stacked[rows : 2 * rows] + below + above


def spread_z(grad):
    return jnp.concatenate([lane_roll(grad, -1), grad, lane_roll(grad, 1)], 0).astype(BF16)


def sigmoid(value):
    return 1.0 / (1.0 + jnp.exp(-value))


def slope(value):
    s = sigmoid(value)
    return s * (1.0 + value * (1.0 - s))


def source_terms(tile, half):
    cell = tile.astype(jnp.int32)
    where_z = jnp.where(cell < 0, -1, cell & 255).astype(F32)
    plane = lax.shift_right_arithmetic(cell, 8)

    def spread(value, row, rows=8):
        return jnp.broadcast_to(value[row : row + 1], (rows, 128))

    at = 4 * half
    z_at = spread(where_z, at + 3, NZ).astype(BF16)
    lanes_z = lax.broadcasted_iota(jnp.int32, (NZ, 128), 0).astype(F32).astype(BF16)
    hot = jnp.where(lanes_z == z_at, jnp.ones((), BF16), jnp.zeros((), BF16))
    plane = spread(plane, at + 3)
    at_x = lax.shift_right_arithmetic(plane, 3)
    at_y = plane & 7
    f = spread(tile, at)
    g = spread(tile, at + 1)
    h = spread(tile, at + 2)
    row = lax.broadcasted_iota(jnp.int32, (8, 128), 0)
    zero = jnp.zeros((8, 128), F32)
    weight_y = jnp.where(row == at_y, 1.0 - g, jnp.where(row == at_y + 1, g, zero))
    last_y = jnp.where(at_y == BY - 1, g, zero)
    weight_x = jnp.where(row == at_x, 1.0 - f, jnp.where(row == at_x + 1, f, zero))
    planes = []
    for i in range(BX + 1):
        here = jnp.where(at_x == i, 1.0 - f, jnp.where(at_x == i - 1, f, zero))
        planes.append(here * weight_y)
    planes.insert(2, weight_x * last_y)
    both = jnp.concatenate(planes, 0)
    tall = jnp.broadcast_to(h[:1], (48, 128))
    upper = both * tall
    lower = both - upper
    joint = jnp.concatenate([lower, upper], 0)
    high = joint.astype(BF16)
    low = (joint - high.astype(F32)).astype(BF16)
    return hot, jnp.concatenate([high, low], 0)


def body(
    cells, offsets, counts, ct, w_first, w_mid_in, w_last_in, w_head_in,
    force, grad_first, grad_mid, grad_last, grad_head,
    packed, got, hot_s, wt_s, dep, dep_in, dens_f, dens, one, two, g_three, g_two, pre_one, pre_two, acc,
    base, w_one, w_mid, w_last, w_mid_t, w_last_t, head_f, head_b, ct_s, pay, half_in, ring, whole,
    send, recv, send_d, recv_d, send_s, recv_s, send_p, recv_p,
):
    n_slab, n_sub = lax.axis_size("slab"), lax.axis_size("sub")
    slab, sub = lax.axis_index("slab"), lax.axis_index("sub")
    up, down, other = (slab + 1) % n_slab, (slab + n_slab - 1) % n_slab, (sub + 1) % n_sub
    neighbours = ((up, sub), (down, sub), (slab, other), (up, other), (down, other))
    devices = n_slab * n_sub
    me = slab * n_sub + sub
    axes = []
    for stride in (1, 4, 16):
        size = min(4, max(1, n_slab // stride))
        at = slab // stride % size
        axes.append((at, [slab + ((at + i) % size - at) * stride for i in range(1, size)]))

    def partner(turn):
        to = (me + turn * SPREAD) % devices
        return (to // n_sub, to % n_sub), to

    barrier = pltpu.get_barrier_semaphore()

    def greet(turn, carry):
        pl.semaphore_signal(barrier, inc=1, device_id=partner(turn)[0], device_id_type=MESH)
        return carry

    lax.fori_loop(1, devices, greet, 0)

    diagonal = lax.broadcasted_iota(jnp.int32, (devices, devices), 0) == lax.broadcasted_iota(
        jnp.int32, (devices, devices), 1
    )
    used = jnp.broadcast_to(counts[...].astype(F32), (devices, devices))
    used = jnp.sum(jnp.where(diagonal, used, 0.0), 1, keepdims=True)
    slot = lax.broadcasted_iota(jnp.int32, (devices, 256), 1).astype(F32)
    live = jnp.where(slot < used, cells[0].astype(F32), -1.0)
    for first in range(0, devices, 8):
        for half in range(2):
            rows = pl.ds(first * 8 + 4 * half + 3, 8, stride=8)
            packed[rows, :] = live[first : first + 8, half * 128 : half * 128 + 128]

    def pack(step, carry):
        for k in range(8):
            to = step * 8 + k
            for half in range(2):
                rows = pl.ds(to * 8 + 4 * half, 3)
                packed[rows, :] = offsets[0, to, :, half * 128 : half * 128 + 128]
        return carry

    lax.fori_loop(0, devices // 8, pack, 0)

    make_tables(w_first, w_mid_in, w_last_in, w_head_in, base, w_one, w_mid, w_last, w_mid_t,
                w_last_t, head_f, head_b)
    ct_s[...] = jnp.zeros_like(ct_s)
    for k in range(3):
        for x in range(BX):
            at = (k * BX + x) * BY
            ct_s[at : at + BY] = ct[k, x]

    def remote(src, dst, at, device, sends, recvs):
        return pltpu.make_async_remote_copy(
            src_ref=src, dst_ref=dst, send_sem=sends.at[at], recv_sem=recvs.at[at],
            device_id=device, device_id_type=MESH,
        )

    pl.semaphore_wait(barrier, devices - 1)

    def tile_rows(at):
        return pl.ds(pl.multiple_of(at * 8, 8), 8)

    def tile_copy(turn):
        device, to = partner(turn)
        return remote(
            packed.at[tile_rows(to)], got.at[tile_rows(turn)], turn, device, send_p, recv_p
        )

    def send_tile(turn, carry):
        tile_copy(turn).start()
        return carry

    lax.fori_loop(1, devices, send_tile, 0)
    got[:8] = packed[tile_rows(me)]

    def take(turn, carry):
        tile_copy(turn).wait_recv()
        return carry

    def gather(step, total):
        lax.fori_loop(jnp.maximum(step * 2 * GROUP, 1), (step + 1) * 2 * GROUP, take, 0)
        for part in range(2):
            for k in range(GROUP):
                tile = got[tile_rows(step * 2 * GROUP + part * GROUP + k)]
                for half in range(2):
                    hot, weights = source_terms(tile, half)
                    at = k * 256 + half * 128
                    hot_s[part, :, at : at + 128] = hot
                    wt_s[part, :, at : at + 128] = weights
            result = dot_nt(wt_s[part], hot_s[part])
            total = total + result[:96] + result[96:]
        return total

    dep2 = lax.fori_loop(0, devices // (2 * GROUP), gather, jnp.zeros((96, NZ), F32))
    dep[...] = dep2[:48] + lane_roll(dep2[48:], 1)

    def sent(turn, carry):
        tile_copy(turn).wait_send()
        return carry

    lax.fori_loop(1, devices, sent, 0)

    upper_rows, lower_rows = pl.ds(16, 32), pl.ds(0, 24)
    copies = []
    for at, (device, rows) in enumerate(
        zip(neighbours, (upper_rows, lower_rows, pl.ds(0, 48), upper_rows, lower_rows))
    ):
        copies.append(remote(dep.at[rows], dep_in.at[at, rows], at, device, send_d, recv_d))
    for copy in copies:
        copy.start()

    dens_f[...] = jnp.zeros_like(dens_f)

    def place(source, source_x, x):
        base = (x + 2) * 16
        dens_f[base + 2 : base + 10] += source[X_ROW[source_x] : X_ROW[source_x] + 8]
        dens_f[base + 10 : base + 11] += source[16 + source_x : 17 + source_x]

    def place_other(source, source_x, x):
        base, row = (x + 2) * 16, X_ROW[source_x]
        dens_f[base : base + 2] += source[row + 6 : row + 8]
        dens_f[base + 2 : base + 3] += source[16 + source_x : 17 + source_x]
        dens_f[base + 10 : base + 12] += source[row : row + 2]

    for x in range(BX + 1):
        place(dep, x, x)
    for copy in copies:
        copy.wait()
    for x in (2, 3, 4):
        place(dep_in.at[0], x, x - 4)
    for x in (0, 1):
        place(dep_in.at[1], x, x + 4)
    for x in range(BX + 1):
        place_other(dep_in.at[2], x, x)
    for x in (2, 3, 4):
        place_other(dep_in.at[3], x, x - 4)
    for x in (0, 1):
        place_other(dep_in.at[4], x, x + 4)
    dens[...] = dens_f[...].astype(BF16)

    for y in range(BY + 2):
        taps = lane_roll(w_one[...], y).astype(BF16)
        pre = join_z(dot(taps, dens[...]))
        one[y] = (pre * sigmoid(pre)).astype(BF16)
        if 1 <= y <= BY:
            pre_one[y - 1] = pre[CORE]

    def rims(field, base):
        right, left = pl.ds(BX * CH, CH), pl.ds(CH, CH)
        before, after = pl.ds(0, CH), pl.ds((BX + 1) * CH, CH)
        core, ys = pl.ds(CH, BX * CH), pl.ds(1, BY)
        plan = (
            ((up, sub), (ys, right), (ys, before)),
            ((down, sub), (ys, left), (ys, after)),
            ((slab, other), (1, core), (BY + 1, core)),
            ((slab, other), (BY, core), (0, core)),
            ((up, other), (1, right), (BY + 1, before)),
            ((up, other), (BY, right), (0, before)),
            ((down, other), (1, left), (BY + 1, after)),
            ((down, other), (BY, left), (0, after)),
        )
        started = []
        for at, (device, src, dst) in enumerate(plan):
            copy = remote(field.at[src], field.at[dst], base + at, device, send, recv)
            copy.start()
            started.append(copy)
        return started

    def planes(field, y):
        return field[y : y + 3].reshape(3 * COLS, NZ)

    def conv(taps, field, y):
        return join_z(dot(taps[...], planes(field, y)))

    for y in range(BY):
        pre = conv(w_mid, one, y)
        pre_two[y] = pre
        two[y + 1, CORE] = (pre * sigmoid(pre)).astype(BF16)
    for copy in rims(two, 0):
        copy.wait()

    row_y = lax.broadcasted_iota(jnp.int32, (128, 128), 0) % BY
    lane_y = lax.broadcasted_iota(jnp.int32, (128, 128), 1) % BY
    out = jnp.zeros((96, NZ), F32)
    head = jnp.zeros((128, 128), F32)
    for y in range(BY):
        pre = conv(w_last, two, y)
        s = sigmoid(pre)
        features = jnp.concatenate([(pre * s).astype(BF16), one[y + 1, CORE]], 0)
        taps = jnp.where(row_y == y, head_f[...], 0.0)[:96].astype(BF16)
        out = out + dot(taps, features)
        head = head + jnp.where(row_y == y, dot_nt(ct_s[...], features), 0.0)
        taps = jnp.where(lane_y == y, head_b[...], 0.0)[: BX * CH].astype(BF16)
        back = dot(taps, ct_s[...])
        g_three[y + 1, CORE] = (back * (s * (1.0 + pre * (1.0 - s)))).astype(BF16)
    started = rims(g_three, 8)
    for k in range(3):
        for x in range(BX):
            at = (k * BX + x) * BY
            force[k, x] = out[at : at + BY].astype(BF16)

    def weight_grad(grads, field, shift):
        acc[:, 3 * COLS :] = jnp.zeros((192, 96), F32)
        for y in range(BY):
            term = dot_nt(spread_z(grads[y + 1, CORE].astype(F32)), planes(field, y))
            if y == 0:
                acc[:, : 3 * COLS] = term
            else:
                acc[:, : 3 * COLS] += term
        rows = []
        for dz in range(3):
            total = jnp.zeros((CH, 384), F32)
            for x in range(BX):
                at = (dz * BX + x) * CH
                total = total + lane_roll(acc[at : at + CH], -CH * x)
            rows.append(total)
        joint = jnp.concatenate(rows, 0)
        lane = lax.broadcasted_iota(jnp.int32, joint.shape, 1)
        joint = jnp.where((lane % 96 < 48) & (lane < 3 * COLS), joint, 0.0)
        return lane_roll(joint, shift) if shift else joint

    sums = weight_grad(g_three, two, 48)
    for copy in started:
        copy.wait()

    for y in range(BY):
        back = conv(w_last_t, g_three, y)
        g_two[y + 1, CORE] = (back * slope(pre_two[y])).astype(BF16)
    started = rims(g_two, 16)
    sums = sums + weight_grad(g_two, one, 0)
    for copy in started:
        copy.wait()

    first = jnp.zeros((192, 128), F32)
    for y in range(BY):
        taps = jnp.where(lane_y == y, head_b[...], 0.0)[BX * CH :].astype(BF16)
        back = conv(w_mid_t, g_two, y) + dot(taps, ct_s[...])
        grad = (back * slope(pre_one[y])).astype(BF16).astype(F32)
        first = first + lane_roll(dot_nt(spread_z(grad), dens[...]), -y)
    rows = []
    for dz in range(3):
        total = jnp.zeros((CH, 128), F32)
        for x in range(BX):
            at = (dz * BX + x) * CH
            total = total + lane_roll(first[at : at + CH], -(16 * x + 17))
        rows.append(total)
    joint = jnp.concatenate(rows, 0)
    lane = lax.broadcasted_iota(jnp.int32, joint.shape, 1)
    joint = jnp.where((lane % 16 < 3) & (lane < 48), joint, 0.0)
    extra = lane_roll(joint, 32)
    row = lax.broadcasted_iota(jnp.int32, (128, 128), 0)
    lane = lax.broadcasted_iota(jnp.int32, (128, 128), 1)
    head = jnp.where(lane % 64 // CH == row // BY % BX, head, 0.0)
    kept = jnp.concatenate(
        [jnp.sum(head[k * 32 : k * 32 + 32], 0, keepdims=True) for k in range(3)]
        + [jnp.zeros((5, 128), F32)],
        0,
    )
    kept = kept + lane_roll(kept, -2 * CH)
    kept = kept + lane_roll(kept, -CH)
    lane = lax.broadcasted_iota(jnp.int32, (8, 128), 1)
    top = jnp.where(lane < CH, kept, 0.0) + jnp.where(
        (lane >= CH) & (lane < 2 * CH), lane_roll(kept, -48), 0.0
    )
    top = lane_roll(top, 80)
    pay[...] = sums
    pay[:, 256:384] += extra
    pay[:8, 256:384] += top

    theirs = pl.ds(pl.multiple_of(other * 24, 8), 24)
    mine = pl.ds(pl.multiple_of(sub * 24, 8), 24)
    copy = remote(pay.at[theirs], half_in, 0, (slab, other), send_s, recv_s)
    copy.start()
    copy.wait()
    total = pay[mine] + half_in[...]
    at_sem = 1
    for turn in range(3):
        copies = []
        for part in range(3):
            at, peers = axes[(part + turn) % 3]
            rows = pl.ds(part * 8, 8)
            ring[turn, at, rows] = total[part * 8 : part * 8 + 8]
            for peer in peers:
                slot = ring.at[turn, at, rows]
                copies.append(remote(slot, slot, at_sem, (peer, sub), send_s, recv_s))
                copies[-1].start()
                at_sem += 1
        for copy in copies:
            copy.wait()
        parts = []
        for part in range(3):
            size = len(axes[(part + turn) % 3][1]) + 1
            rows = slice(part * 8, part * 8 + 8)
            value = ring[turn, 0, rows]
            for slot in range(1, size):
                value = value + ring[turn, slot, rows]
            parts.append(value)
        total = jnp.concatenate(parts, 0)
    whole[mine] = total * (1.0 / math.sqrt(BX * n_slab * BY * n_sub * NZ))
    copy = remote(whole.at[mine], whole.at[mine], at_sem, (slab, other), send_s, recv_s)
    copy.start()
    copy.wait()
    for dx, dy, dz in OFFSETS:
        rows, tap = slice(dz * CH, dz * CH + CH), dx * 9 + dy * 3 + dz
        at, to = dy * 96 + dx * CH, slice(tap * CH, tap * CH + CH)
        grad_mid[:, to] = whole[rows, at : at + CH]
        grad_last[:, to] = whole[rows, at + 48 : at + 48 + CH]
        at = 288 + dx * CH + dy
        grad_first[:, tap : tap + 1] = whole[rows, at : at + 1]
    grad_head[...] = whole[:3, 336:368]


OFFSETS = [(dx, dy, dz) for dx in range(3) for dy in range(3) for dz in range(3)]


def make_tables(w_first, w_mid, w_last, w_head, base, one, mid, last, mid_t, last_t, head_f, head_b):
    def spread(out):
        for dz in range(3):
            for x in range(BX):
                at = (dz * BX + x) * CH
                moved = lane_roll(base[dz * CH : dz * CH + CH], x * CH)
                out[at : at + CH] = moved[:, : 3 * COLS].astype(BF16)

    base[...] = jnp.zeros_like(base)
    for source, out, out_t in ((w_mid, mid, mid_t), (w_last, last, last_t)):
        weights = source[...].astype(F32)
        for dx, dy, dz in OFFSETS:
            tap, at = dx * 9 + dy * 3 + dz, dy * 96 + dx * CH
            base[dz * CH : dz * CH + CH, at : at + CH] = weights[:, tap * CH : tap * CH + CH]
        spread(out)
        padded = jnp.concatenate([weights, jnp.zeros((CH, 80), F32)], 1)
        turned = jnp.concatenate([padded, jnp.zeros((112, 512), F32)], 0).T
        for dx, dy, dz in OFFSETS:
            tap, at = dx * 9 + dy * 3 + dz, (2 - dy) * 96 + (2 - dx) * CH
            to = (2 - dz) * CH
            base[to : to + CH, at : at + CH] = turned[tap * CH : tap * CH + CH, :CH]
        spread(out_t)
    base[...] = jnp.zeros_like(base)
    weights = w_first[...].astype(F32)
    for dx, dy, dz in OFFSETS:
        tap, at = dx * 9 + dy * 3 + dz, dx * 16 + dy
        base[dz * CH : dz * CH + CH, at : at + 1] = weights[:, tap : tap + 1]
    for dz in range(3):
        for x in range(BX + 2):
            at = (dz * (BX + 2) + x) * CH
            one[at : at + CH] = lane_roll(base[dz * CH : dz * CH + CH, :128], x * 16)
    head_f[...] = jnp.zeros_like(head_f)
    weights = w_head[...].astype(F32)
    for k in range(3):
        for x in range(BX):
            at = (k * BX + x) * BY
            for half in range(2):
                row = weights[k : k + 1, half * CH : half * CH + CH]
                to = half * 64 + x * CH
                head_f[at : at + BY, to : to + CH] = jnp.broadcast_to(row, (BY, CH))
    head_b[...] = head_f[...].T


def per_device(part_cells, part_offsets, part_counts, w_first, w_mid, w_last, w_head, cotangent):
    devices = part_counts.shape[1]
    vmem = pl.BlockSpec(memory_space=pltpu.VMEM)
    field = pltpu.VMEM((BY + 2, COLS, NZ), BF16)
    kept = pltpu.VMEM((BY, BX * CH, NZ), F32)
    table = pltpu.VMEM((192, 3 * COLS), BF16)
    return pl.pallas_call(
        body,
        out_shape=(
            jax.ShapeDtypeStruct(cotangent.shape, BF16),
            jax.ShapeDtypeStruct(w_first.shape, F32),
            jax.ShapeDtypeStruct(w_mid.shape, F32),
            jax.ShapeDtypeStruct(w_last.shape, F32),
            jax.ShapeDtypeStruct(w_head.shape, F32),
        ),
        in_specs=[vmem] * 8,
        out_specs=[vmem] * 5,
        scratch_shapes=[
            pltpu.VMEM((devices * 8, 128), F32),
            pltpu.VMEM((devices * 8, 128), F32),
            pltpu.VMEM((2, NZ, 256 * GROUP), BF16),
            pltpu.VMEM((2, 192, 256 * GROUP), BF16),
            pltpu.VMEM((48, NZ), F32),
            pltpu.VMEM((5, 48, NZ), F32),
            pltpu.VMEM((128, NZ), F32),
            pltpu.VMEM((128, NZ), BF16),
            field, field, field, field, kept, kept,
            pltpu.VMEM((192, 384), F32),
            pltpu.VMEM((48, 384), F32),
            pltpu.VMEM((288, 128), F32),
            table, table, table, table,
            pltpu.VMEM((128, 128), F32),
            pltpu.VMEM((128, 128), F32),
            pltpu.VMEM((128, NZ), BF16),
            pltpu.VMEM((48, 384), F32),
            pltpu.VMEM((24, 384), F32),
            pltpu.VMEM((3, 4, 24, 384), F32),
            pltpu.VMEM((48, 384), F32),
            pltpu.SemaphoreType.DMA((24,)),
            pltpu.SemaphoreType.DMA((24,)),
            pltpu.SemaphoreType.DMA((5,)),
            pltpu.SemaphoreType.DMA((5,)),
            pltpu.SemaphoreType.DMA((29,)),
            pltpu.SemaphoreType.DMA((29,)),
            pltpu.SemaphoreType.DMA((devices,)),
            pltpu.SemaphoreType.DMA((devices,)),
        ],
        compiler_params=pltpu.CompilerParams(
            collective_id=0, has_side_effects=True, vmem_limit_bytes=48 << 20
        ),
        name="level",
    )(part_cells, part_offsets, part_counts, cotangent, w_first, w_mid, w_last, w_head)


def solution(mesh):
    in_specs = (
        P(("slab", "sub"), None, None),
        P(("slab", "sub"), None, None, None),
        P(("slab", "sub"), None),
        P(), P(), P(), P(),
        P(None, "slab", "sub", None),
    )
    out_specs = (P(None, "slab", "sub", None), P(), P(), P(), P())
    return jax.shard_map(
        per_device, mesh=mesh, in_specs=in_specs, out_specs=out_specs, check_vma=False
    )
```

```python
import functools
import math

import jax
import jax.numpy as jnp
from jax import lax
from jax.experimental import pallas as pl
from jax.experimental.pallas import tpu as pltpu
from jax.sharding import PartitionSpec as P

MESH = pl.DeviceIdType.MESH
F32 = jnp.float32
BF16 = jnp.bfloat16

BX, BY, NZ, CH = 4, 8, 256, 16
COLS = (BX + 2) * CH
CORE = slice(CH, CH + BX * CH)
GROUP = 4
X_ROW = (0, 8, 24, 32, 40)


def lane_roll(value, shift):
    return pltpu.roll(value, shift % value.shape[1], 1)


def dot(a, b):
    return jnp.dot(a, b, preferred_element_type=F32)


def dot_nt(a, b):
    return lax.dot_general(a, b, (((1,), (1,)), ((), ())), preferred_element_type=F32)


def join_z(stacked):
    rows = stacked.shape[0] // 3
    below = lane_roll(stacked[:rows], 1)
    above = lane_roll(stacked[2 * rows :], -1)
    return stacked[rows : 2 * rows] + below + above


def spread_z(grad):
    return jnp.concatenate([lane_roll(grad, -1), grad, lane_roll(grad, 1)], 0).astype(BF16)


def sigmoid(value):
    return 1.0 / (1.0 + jnp.exp(-value))


def slope(value):
    s = sigmoid(value)
    return s * (1.0 + value * (1.0 - s))


def source_terms(tile, half):
    cell = tile.astype(jnp.int32)
    where_z = jnp.where(cell < 0, -1, cell & 255).astype(F32)
    plane = lax.shift_right_arithmetic(cell, 8)

    def spread(value, row, rows=8):
        return jnp.broadcast_to(value[row : row + 1], (rows, 128))

    at = 4 * half
    z_at = spread(where_z, at + 3, NZ).astype(BF16)
    lanes_z = lax.broadcasted_iota(jnp.int32, (NZ, 128), 0).astype(F32).astype(BF16)
    hot = jnp.where(lanes_z == z_at, jnp.ones((), BF16), jnp.zeros((), BF16))
    plane = spread(plane, at + 3)
    at_x = lax.shift_right_arithmetic(plane, 3)
    at_y = plane & 7
    f = spread(tile, at)
    g = spread(tile, at + 1)
    h = spread(tile, at + 2)
    row = lax.broadcasted_iota(jnp.int32, (8, 128), 0)
    zero = jnp.zeros((8, 128), F32)
    weight_y = jnp.where(row == at_y, 1.0 - g, jnp.where(row == at_y + 1, g, zero))
    last_y = jnp.where(at_y == BY - 1, g, zero)
    weight_x = jnp.where(row == at_x, 1.0 - f, jnp.where(row == at_x + 1, f, zero))
    planes = []
    for i in range(BX + 1):
        here = jnp.where(at_x == i, 1.0 - f, jnp.where(at_x == i - 1, f, zero))
        planes.append(here * weight_y)
    planes.insert(2, weight_x * last_y)
    both = jnp.concatenate(planes, 0)
    tall = jnp.broadcast_to(h[:1], (48, 128))
    upper = both * tall
    lower = both - upper
    joint = jnp.concatenate([lower, upper], 0)
    high = joint.astype(BF16)
    low = (joint - high.astype(F32)).astype(BF16)
    return hot, jnp.concatenate([high, low], 0)


def body(
    cells_hbm, offsets_hbm, counts, ct_hbm, w_first, w_mid_in, w_last_in, w_head_in,
    force, sums,
    cells, offsets, ct_own, ct_in, force_s,
    packed, got, hot_s, wt_s, dep, dep_in, dens_f, dens, one, two, g_three, g_two, pre_one, pre_two, acc,
    base, w_one, w_mid, w_last, w_mid_t, w_last_t, head_f, head_b, ct_s,
    pay, half_in, ring, tile, tile_in, tiles,
    load, send, recv, send_d, recv_d, send_s, recv_s, send_p, recv_p, send_f, recv_f, send_m, recv_m,
):
    n_slab, n_sub = lax.axis_size("slab"), lax.axis_size("sub")
    slab, sub = lax.axis_index("slab"), lax.axis_index("sub")
    devices = n_slab * n_sub
    me = slab * n_sub + sub
    other = (sub + 1) % n_sub
    stop = ring_stop(slab)
    up, down = ring_slab((stop + 1) % n_slab), ring_slab((stop + n_slab - 1) % n_slab)
    neighbours = ((up, sub), (down, sub), (slab, other), (up, other), (down, other))
    worker, owner = (ring_slab(slab), other), (stop, other)
    axes = []
    for stride in (1, 4, 16):
        size = min(4, max(1, n_slab // stride))
        at = slab // stride % size
        axes.append((at, [slab + ((at + i) % size - at) * stride for i in range(1, size)]))

    loads = [
        pltpu.make_async_copy(src, dst, load.at[at])
        for at, (src, dst) in enumerate(
            ((cells_hbm.at[0], cells), (offsets_hbm.at[0], offsets), (ct_hbm, ct_own))
        )
    ]
    for copy in loads:
        copy.start()

    def partner(turn):
        to = (me + turn) % devices
        return (to // n_sub, to % n_sub), ring_stop(to // n_sub) * n_sub + (to + 1) % n_sub

    barrier = pltpu.get_barrier_semaphore()

    def greet(turn, carry):
        pl.semaphore_signal(barrier, inc=1, device_id=partner(turn)[0], device_id_type=MESH)
        return carry

    lax.fori_loop(1, devices, greet, 0)
    make_tables(w_first, w_mid_in, w_last_in, w_head_in, base, w_one, w_mid, w_last, w_mid_t,
                w_last_t, head_f, head_b)
    for copy in loads:
        copy.wait()

    diagonal = lax.broadcasted_iota(jnp.int32, (devices, devices), 0) == lax.broadcasted_iota(
        jnp.int32, (devices, devices), 1
    )
    used = jnp.broadcast_to(counts[...].astype(F32), (devices, devices))
    used = jnp.sum(jnp.where(diagonal, used, 0.0), 1, keepdims=True)
    slot = lax.broadcasted_iota(jnp.int32, (devices, 256), 1).astype(F32)
    live = jnp.where(slot < used, cells[...].astype(F32), -1.0)
    for first in range(0, devices, 8):
        for half in range(2):
            rows = pl.ds(first * 8 + 4 * half + 3, 8, stride=8)
            packed[rows, :] = live[first : first + 8, half * 128 : half * 128 + 128]

    def pack(step, carry):
        for k in range(8):
            to = step * 8 + k
            for half in range(2):
                rows = pl.ds(to * 8 + 4 * half, 3)
                packed[rows, :] = offsets[to, :, half * 128 : half * 128 + 128]
        return carry

    lax.fori_loop(0, devices // 8, pack, 0)

    def remote(src, dst, at, device, sends, recvs):
        return pltpu.make_async_remote_copy(
            src_ref=src, dst_ref=dst, send_sem=sends.at[at], recv_sem=recvs.at[at],
            device_id=device, device_id_type=MESH,
        )

    pl.semaphore_wait(barrier, devices - 1)

    def tile_rows(at):
        return pl.ds(pl.multiple_of(at * 8, 8), 8)

    def send_tile(turn, carry):
        device, brick = partner(turn)
        remote(
            packed.at[tile_rows(brick)], got.at[tile_rows(turn)], turn // (2 * GROUP), device,
            send_p, recv_p,
        ).start()
        return carry

    lax.fori_loop(1, devices, send_tile, 0)
    got[:8] = packed[tile_rows(partner(0)[1])]
    ct_copy = remote(ct_own, ct_in, 0, worker, send_f, recv_f)
    ct_copy.start()

    def arrived(step, tiles_in):
        rows = pl.ds(0, tiles_in * 8)
        return pltpu.make_async_copy(got.at[rows], got.at[rows], recv_p.at[step])

    def left(step, tiles_out):
        rows = pl.ds(0, tiles_out * 8)
        return pltpu.make_async_copy(packed.at[rows], packed.at[rows], send_p.at[step])

    def gather(step, total):
        for part in range(2):
            for k in range(GROUP):
                source = got[tile_rows(step * 2 * GROUP + part * GROUP + k)]
                for half in range(2):
                    hot, weights = source_terms(source, half)
                    at = k * 256 + half * 128
                    hot_s[part, :, at : at + 128] = hot
                    wt_s[part, :, at : at + 128] = weights
            result = dot_nt(wt_s[part], hot_s[part])
            total = total + result[:96] + result[96:]
        return total

    def wait_and_gather(step, total):
        arrived(step, 2 * GROUP).wait()
        return gather(step, total)

    arrived(0, 2 * GROUP - 1).wait()
    dep2 = gather(0, jnp.zeros((96, NZ), F32))
    dep2 = lax.fori_loop(1, devices // (2 * GROUP), wait_and_gather, dep2)
    dep[...] = dep2[:48] + lane_roll(dep2[48:], 1)
    left(0, 2 * GROUP - 1).wait()

    def sent(step, carry):
        left(step, 2 * GROUP).wait()
        return carry

    lax.fori_loop(1, devices // (2 * GROUP), sent, 0)

    upper_rows, lower_rows = pl.ds(16, 32), pl.ds(0, 24)
    copies = []
    for at, (device, rows) in enumerate(
        zip(neighbours, (upper_rows, lower_rows, pl.ds(0, 48), upper_rows, lower_rows))
    ):
        copies.append(remote(dep.at[rows], dep_in.at[at, rows], at, device, send_d, recv_d))
    for copy in copies:
        copy.start()

    dens_f[...] = jnp.zeros_like(dens_f)

    def place(source, source_x, x):
        base = (x + 2) * 16
        dens_f[base + 2 : base + 10] += source[X_ROW[source_x] : X_ROW[source_x] + 8]
        dens_f[base + 10 : base + 11] += source[16 + source_x : 17 + source_x]

    def place_other(source, source_x, x):
        base, row = (x + 2) * 16, X_ROW[source_x]
        dens_f[base : base + 2] += source[row + 6 : row + 8]
        dens_f[base + 2 : base + 3] += source[16 + source_x : 17 + source_x]
        dens_f[base + 10 : base + 12] += source[row : row + 2]

    for x in range(BX + 1):
        place(dep, x, x)
    for copy in copies:
        copy.wait()
    for x in (2, 3, 4):
        place(dep_in.at[0], x, x - 4)
    for x in (0, 1):
        place(dep_in.at[1], x, x + 4)
    for x in range(BX + 1):
        place_other(dep_in.at[2], x, x)
    for x in (2, 3, 4):
        place_other(dep_in.at[3], x, x - 4)
    for x in (0, 1):
        place_other(dep_in.at[4], x, x + 4)
    dens[...] = dens_f[...].astype(BF16)

    for y in range(BY + 2):
        taps = lane_roll(w_one[...], y).astype(BF16)
        pre = join_z(dot(taps, dens[...]))
        one[y] = (pre * sigmoid(pre)).astype(BF16)
        if 1 <= y <= BY:
            pre_one[y - 1] = pre[CORE]

    right, left_end = pl.ds(BX * CH, CH), pl.ds(CH, CH)
    before, after = pl.ds(0, CH), pl.ds((BX + 1) * CH, CH)
    core = pl.ds(CH, BX * CH)

    def rims(field, base, part):
        ys = pl.ds(1 + part * (BY // 2), BY // 2)
        edge, to = (1, BY + 1) if part == 0 else (BY, 0)
        plan = (
            ((slab, other), (edge, core), (to, core)),
            ((up, other), (edge, right), (to, before)),
            ((down, other), (edge, left_end), (to, after)),
            ((up, sub), (ys, right), (ys, before)),
            ((down, sub), (ys, left_end), (ys, after)),
        )
        started = []
        for at, (device, src, dst) in enumerate(plan):
            place = base + part * len(plan) + at
            copy = remote(field.at[src], field.at[dst], place, device, send, recv)
            copy.start()
            started.append(copy)
        return started

    def planes(field, y):
        return field[y : y + 3].reshape(3 * COLS, NZ)

    def conv(taps, field, y):
        return join_z(dot(taps[...], planes(field, y)))

    started = []
    for y in range(BY):
        pre = conv(w_mid, one, y)
        pre_two[y] = pre
        two[y + 1, CORE] = (pre * sigmoid(pre)).astype(BF16)
        if y % 4 == 3:
            started += rims(two, 0, y // 4)
    ct_copy.wait()
    ct_s[...] = jnp.zeros_like(ct_s)
    for k in range(3):
        for x in range(BX):
            at = (k * BX + x) * BY
            ct_s[at : at + BY] = ct_in[k, x]
    for copy in started:
        copy.wait()

    row_y = lax.broadcasted_iota(jnp.int32, (128, 128), 0) % BY
    lane_y = lax.broadcasted_iota(jnp.int32, (128, 128), 1) % BY
    out = jnp.zeros((96, NZ), F32)
    head = jnp.zeros((128, 128), F32)
    started = []
    for y in range(BY):
        pre = conv(w_last, two, y)
        s = sigmoid(pre)
        features = jnp.concatenate([(pre * s).astype(BF16), one[y + 1, CORE]], 0)
        taps = jnp.where(row_y == y, head_f[...], 0.0)[:96].astype(BF16)
        out = out + dot(taps, features)
        head = head + jnp.where(row_y == y, dot_nt(ct_s[...], features), 0.0)
        taps = jnp.where(lane_y == y, head_b[...], 0.0)[: BX * CH].astype(BF16)
        back = dot(taps, ct_s[...])
        g_three[y + 1, CORE] = (back * (s * (1.0 + pre * (1.0 - s)))).astype(BF16)
        if y % 4 == 3:
            started += rims(g_three, 10, y // 4)
    for k in range(3):
        for x in range(BX):
            at = (k * BX + x) * BY
            force_s[k, x] = out[at : at + BY].astype(BF16)
    force_copy = remote(force_s, force, 1, owner, send_f, recv_f)
    force_copy.start()

    def weight_grad(grads, field, out):
        acc[:, 3 * COLS :] = jnp.zeros((192, 96), F32)
        for y in range(BY):
            term = dot_nt(spread_z(grads[y + 1, CORE].astype(F32)), planes(field, y))
            if y == 0:
                acc[:, : 3 * COLS] = term
            else:
                acc[:, : 3 * COLS] += term
        rows = []
        for dz in range(3):
            total = jnp.zeros((CH, 384), F32)
            for x in range(BX):
                at = (dz * BX + x) * CH
                total = total + lane_roll(acc[at : at + CH], -CH * x)
            rows.append(total)
        joint = jnp.concatenate(rows, 0)
        lane = lax.broadcasted_iota(jnp.int32, joint.shape, 1)
        joint = jnp.where((lane % 96 < 48) & (lane < 3 * COLS), joint, 0.0)
        moved = [jnp.where(lane < 48, joint, 0.0)]
        for dy in (1, 2):
            inside = (lane >= 48 * dy) & (lane < 48 * dy + 48)
            moved.append(jnp.where(inside, lane_roll(joint, -48 * dy), 0.0))
        joint = moved[0] + moved[1] + moved[2]
        out[:48] = joint[:, :128]
        tail = joint[:CH, 128:256]
        for dz in (1, 2):
            tail = tail + lane_roll(joint[dz * CH : dz * CH + CH, 128:256], dz * CH)
        out[48:] = tail

    theirs = pl.ds(pl.multiple_of(other * 32, 8), 32)
    mine = pl.ds(pl.multiple_of(sub * 32, 8), 32)

    class Sum:
        def __init__(self, at):
            self.at, self.next, self.copies = at, at * 38, []

        def begin(self, src, dst, device):
            self.copies.append(remote(src, dst, self.next, device, send_s, recv_s))
            self.copies[-1].start()
            self.next += 1

        def end(self):
            for copy in self.copies:
                copy.wait()
            self.copies = []

        def across(self):
            self.begin(pay.at[self.at, theirs], half_in.at[self.at], (slab, other))

        def joined(self):
            self.end()
            return pay[self.at, mine] + half_in[self.at]

        def out(self, turn, total):
            for part in range(4):
                at, peers = axes[(part + turn) % 3]
                rows = pl.ds(part * 8, 8)
                ring[self.at, turn, at, rows] = total[part * 8 : part * 8 + 8]
                for peer in peers:
                    slot = ring.at[self.at, turn, at, rows]
                    self.begin(slot, slot, (peer, sub))

        def back(self, turn):
            self.end()
            parts = []
            for part in range(4):
                rows = slice(part * 8, part * 8 + 8)
                value = ring[self.at, turn, 0, rows]
                for slot in range(1, len(axes[(part + turn) % 3][1]) + 1):
                    value = value + ring[self.at, turn, slot, rows]
                parts.append(value)
            return jnp.concatenate(parts, 0)

        def share(self, total):
            rows = pl.ds(pl.multiple_of(self.at * 64 + sub * 32, 8), 32)
            sums[rows] = total * scale
            self.begin(sums.at[rows], sums.at[rows], (slab, other))

    scale = 1.0 / math.sqrt(BX * n_slab * BY * n_sub * NZ)
    sum_last, sum_mid = Sum(0), Sum(1)

    weight_grad(g_three, two, pay.at[0])
    row = lax.broadcasted_iota(jnp.int32, (128, 128), 0)
    lane = lax.broadcasted_iota(jnp.int32, (128, 128), 1)
    head = jnp.where(lane % 64 // CH == row // BY % BX, head, 0.0)
    kept = jnp.concatenate(
        [jnp.sum(head[k * 32 : k * 32 + 32], 0, keepdims=True) for k in range(3)]
        + [jnp.zeros((5, 128), F32)],
        0,
    )
    kept = kept + lane_roll(kept, -2 * CH)
    kept = kept + lane_roll(kept, -CH)
    lane = lax.broadcasted_iota(jnp.int32, (8, 128), 1)
    top = jnp.where(lane < CH, kept, 0.0) + jnp.where(
        (lane >= CH) & (lane < 2 * CH), lane_roll(kept, -48), 0.0
    )
    pay[0, 48:56] += lane_roll(top, 48)
    sum_last.across()
    for copy in started:
        copy.wait()

    started = []
    for y in range(BY):
        back = conv(w_last_t, g_three, y)
        g_two[y + 1, CORE] = (back * slope(pre_two[y])).astype(BF16)
        if y % 4 == 3:
            started += rims(g_two, 20, y // 4)
    sum_last.out(0, sum_last.joined())
    weight_grad(g_two, one, pay.at[1])
    sum_mid.across()
    sum_last.out(1, sum_last.back(0))
    for copy in started:
        copy.wait()
    sum_mid.out(0, sum_mid.joined())

    first = jnp.zeros((192, 128), F32)
    for y in range(BY):
        taps = jnp.where(lane_y == y, head_b[...], 0.0)[BX * CH :].astype(BF16)
        back = conv(w_mid_t, g_two, y) + dot(taps, ct_s[...])
        grad = (back * slope(pre_one[y])).astype(BF16).astype(F32)
        first = first + lane_roll(dot_nt(spread_z(grad), dens[...]), -y)
    rows = []
    for dz in range(3):
        total = jnp.zeros((CH, 128), F32)
        for x in range(BX):
            at = (dz * BX + x) * CH
            total = total + lane_roll(first[at : at + CH], -(16 * x + 17))
        rows.append(total)
    joint = jnp.concatenate(rows, 0)
    lane = lax.broadcasted_iota(jnp.int32, joint.shape, 1)
    joint = jnp.where((lane % 16 < 3) & (lane < 48), joint, 0.0)
    value = jnp.zeros((8, 128), F32)
    for block, shift in enumerate(BLOCK_LANE):
        value = value + lane_roll(joint[block * 8 : block * 8 + 8], shift)
    tile[...] = value
    tile_copy = remote(tile, tile_in, 2, (slab, other), send_f, recv_f)
    tile_copy.start()
    sum_mid.out(1, sum_mid.back(0))
    sum_last.out(2, sum_last.back(1))
    tile_copy.wait()
    tiles[slab] = tile[...] + tile_in[...]
    if n_slab > 1:

        def spread_tile(turn, carry):
            peer = (slab + 1 + (turn + n_slab * 2 // 3) % (n_slab - 1)) % n_slab
            remote(tiles.at[slab], tiles.at[slab], 0, (peer, sub), send_m, recv_m).start()
            return carry

        lax.fori_loop(0, n_slab - 1, spread_tile, 0)
    sum_mid.out(2, sum_mid.back(1))
    sum_last.share(sum_last.back(2))
    sum_mid.share(sum_mid.back(2))
    if n_slab > 1:
        some = pl.ds(0, n_slab - 1)
        pltpu.make_async_copy(tiles.at[some], tiles.at[some], recv_m.at[0]).wait()
        pltpu.make_async_copy(tiles.at[some], tiles.at[some], send_m.at[0]).wait()
    sums[128:136] = jnp.sum(tiles[...], 0) * scale
    sum_last.end()
    sum_mid.end()
    force_copy.wait()


def ring_stop(slab):
    y = (slab // 4 + slab // 16) % 4
    return slab // 16 * 16 + y * 4 + (slab + y) % 4


def ring_slab(stop):
    z, y = stop // 16, stop // 4 % 4
    return z * 16 + (y + 4 - z) % 4 * 4 + (stop + 4 - y) % 4


def finish(force_in, sums, force, grad_first, grad_mid, grad_last, grad_head):
    force[...] = force_in[...]
    for dx, dy, dz in OFFSETS:
        tap, rows, at = dx * 9 + dy * 3 + dz, dz * CH, dy * 48 + dx * CH
        if at == 128:
            rows, at = 48, dz * CH
        for first, out in ((64, grad_mid), (0, grad_last)):
            block = sums[first + rows : first + rows + CH, at : at + CH]
            out[:, tap * CH : tap * CH + CH] = block
        for half in range(2):
            at = BLOCK_LANE[2 * dz + half] + dx * CH + dy
            grad_first[half * 8 : half * 8 + 8, tap : tap + 1] = sums[128:136, at : at + 1]
    grad_head[...] = sums[48:51, 48:80]


BLOCK_LANE = (0, 3, 6, 9, 12, 48)
OFFSETS = [(dx, dy, dz) for dx in range(3) for dy in range(3) for dz in range(3)]


def make_tables(w_first, w_mid, w_last, w_head, base, one, mid, last, mid_t, last_t, head_f, head_b):
    def spread(out):
        for dz in range(3):
            for x in range(BX):
                at = (dz * BX + x) * CH
                moved = lane_roll(base[dz * CH : dz * CH + CH], x * CH)
                out[at : at + CH] = moved[:, : 3 * COLS].astype(BF16)

    base[...] = jnp.zeros_like(base)
    for source, out, out_t in ((w_mid, mid, mid_t), (w_last, last, last_t)):
        weights = source[...].astype(F32)
        for dx, dy, dz in OFFSETS:
            tap, at = dx * 9 + dy * 3 + dz, dy * 96 + dx * CH
            base[dz * CH : dz * CH + CH, at : at + CH] = weights[:, tap * CH : tap * CH + CH]
        spread(out)
        padded = jnp.concatenate([weights, jnp.zeros((CH, 80), F32)], 1)
        turned = jnp.concatenate([padded, jnp.zeros((112, 512), F32)], 0).T
        for dx, dy, dz in OFFSETS:
            tap, at = dx * 9 + dy * 3 + dz, (2 - dy) * 96 + (2 - dx) * CH
            to = (2 - dz) * CH
            base[to : to + CH, at : at + CH] = turned[tap * CH : tap * CH + CH, :CH]
        spread(out_t)
    base[...] = jnp.zeros_like(base)
    weights = w_first[...].astype(F32)
    for dx, dy, dz in OFFSETS:
        tap, at = dx * 9 + dy * 3 + dz, dx * 16 + dy
        base[dz * CH : dz * CH + CH, at : at + 1] = weights[:, tap : tap + 1]
    for dz in range(3):
        for x in range(BX + 2):
            at = (dz * (BX + 2) + x) * CH
            one[at : at + CH] = lane_roll(base[dz * CH : dz * CH + CH, :128], x * 16)
    head_f[...] = jnp.zeros_like(head_f)
    weights = w_head[...].astype(F32)
    for k in range(3):
        for x in range(BX):
            at = (k * BX + x) * BY
            for half in range(2):
                row = weights[k : k + 1, half * CH : half * CH + CH]
                to = half * 64 + x * CH
                head_f[at : at + BY, to : to + CH] = jnp.broadcast_to(row, (BY, CH))
    head_b[...] = head_f[...].T


def per_device(part_cells, part_offsets, part_counts, w_first, w_mid, w_last, w_head, cotangent):
    devices = part_counts.shape[1]
    vmem = pl.BlockSpec(memory_space=pltpu.VMEM)
    field = pltpu.VMEM((BY + 2, COLS, NZ), BF16)
    kept = pltpu.VMEM((BY, BX * CH, NZ), F32)
    table = pltpu.VMEM((192, 3 * COLS), BF16)
    hbm = pl.BlockSpec(memory_space=pltpu.HBM)
    slots = part_cells.shape[2]
    force, sums = pl.pallas_call(
        body,
        out_shape=(
            jax.ShapeDtypeStruct(cotangent.shape, BF16),
            jax.ShapeDtypeStruct((136, 128), F32),
        ),
        in_specs=[hbm, hbm, vmem, hbm, vmem, vmem, vmem, vmem],
        out_specs=[vmem] * 2,
        scratch_shapes=[
            pltpu.VMEM((devices, slots), jnp.int32),
            pltpu.VMEM((devices, 3, slots), F32),
            pltpu.VMEM(cotangent.shape, BF16),
            pltpu.VMEM(cotangent.shape, BF16),
            pltpu.VMEM(cotangent.shape, BF16),
            pltpu.VMEM((devices * 8, 128), F32),
            pltpu.VMEM((devices * 8, 128), F32),
            pltpu.VMEM((2, NZ, 256 * GROUP), BF16),
            pltpu.VMEM((2, 192, 256 * GROUP), BF16),
            pltpu.VMEM((48, NZ), F32),
            pltpu.VMEM((5, 48, NZ), F32),
            pltpu.VMEM((128, NZ), F32),
            pltpu.VMEM((128, NZ), BF16),
            field, field, field, field, kept, kept,
            pltpu.VMEM((192, 384), F32),
            pltpu.VMEM((48, 384), F32),
            pltpu.VMEM((288, 128), F32),
            table, table, table, table,
            pltpu.VMEM((128, 128), F32),
            pltpu.VMEM((128, 128), F32),
            pltpu.VMEM((128, NZ), BF16),
            pltpu.VMEM((2, 64, 128), F32),
            pltpu.VMEM((2, 32, 128), F32),
            pltpu.VMEM((2, 3, 4, 32, 128), F32),
            pltpu.VMEM((8, 128), F32),
            pltpu.VMEM((8, 128), F32),
            pltpu.VMEM((devices // 2, 8, 128), F32),
            pltpu.SemaphoreType.DMA((3,)),
            pltpu.SemaphoreType.DMA((30,)),
            pltpu.SemaphoreType.DMA((30,)),
            pltpu.SemaphoreType.DMA((5,)),
            pltpu.SemaphoreType.DMA((5,)),
            pltpu.SemaphoreType.DMA((76,)),
            pltpu.SemaphoreType.DMA((76,)),
            pltpu.SemaphoreType.DMA((devices // (2 * GROUP),)),
            pltpu.SemaphoreType.DMA((devices // (2 * GROUP),)),
            pltpu.SemaphoreType.DMA((3,)),
            pltpu.SemaphoreType.DMA((3,)),
            pltpu.SemaphoreType.DMA((1,)),
            pltpu.SemaphoreType.DMA((1,)),
        ],
        compiler_params=pltpu.CompilerParams(
            collective_id=0, has_side_effects=True, vmem_limit_bytes=48 << 20
        ),
        name="level",
    )(part_cells, part_offsets, part_counts, cotangent, w_first, w_mid, w_last, w_head)
    return pl.pallas_call(
        finish,
        out_shape=(
            jax.ShapeDtypeStruct(cotangent.shape, BF16),
            jax.ShapeDtypeStruct(w_first.shape, F32),
            jax.ShapeDtypeStruct(w_mid.shape, F32),
            jax.ShapeDtypeStruct(w_last.shape, F32),
            jax.ShapeDtypeStruct(w_head.shape, F32),
        ),
        in_specs=[vmem] * 2,
        out_specs=[vmem] * 5,
        name="finish",
    )(force, sums)


def solution(mesh):
    in_specs = (
        P(("slab", "sub"), None, None),
        P(("slab", "sub"), None, None, None),
        P(("slab", "sub"), None),
        P(), P(), P(), P(),
        P(None, "slab", "sub", None),
    )
    out_specs = (P(None, "slab", "sub", None), P(), P(), P(), P())
    return jax.shard_map(
        per_device, mesh=mesh, in_specs=in_specs, out_specs=out_specs, check_vma=False
    )
```

```python
import functools
import math

import jax
import jax.numpy as jnp
from jax import lax
from jax.experimental import pallas as pl
from jax.experimental.pallas import tpu as pltpu
from jax.sharding import PartitionSpec as P

MESH = pl.DeviceIdType.MESH
F32 = jnp.float32
BF16 = jnp.bfloat16

BX, BY, NZ, CH = 4, 8, 256, 16
COLS = (BX + 2) * CH
CORE = slice(CH, CH + BX * CH)
GROUP = 4
X_ROW = (0, 8, 24, 32, 40)


def lane_roll(value, shift):
    return pltpu.roll(value, shift % value.shape[1], 1)


def dot(a, b):
    return jnp.dot(a, b, preferred_element_type=F32)


def dot_nt(a, b):
    return lax.dot_general(a, b, (((1,), (1,)), ((), ())), preferred_element_type=F32)


def join_z(stacked):
    rows = stacked.shape[0] // 3
    below = lane_roll(stacked[:rows], 1)
    above = lane_roll(stacked[2 * rows :], -1)
    return stacked[rows : 2 * rows] + below + above


def spread_z(grad):
    return jnp.concatenate([lane_roll(grad, -1), grad, lane_roll(grad, 1)], 0).astype(BF16)


def sigmoid(value):
    return 1.0 / (1.0 + jnp.exp(-value))


def slope(value):
    s = sigmoid(value)
    return s * (1.0 + value * (1.0 - s))


def source_terms(tile, half):
    cell = tile.astype(jnp.int32)
    where_z = jnp.where(cell < 0, -1, cell & 255).astype(F32)
    plane = lax.shift_right_arithmetic(cell, 8)

    def spread(value, row, rows=8):
        return jnp.broadcast_to(value[row : row + 1], (rows, 128))

    at = 4 * half
    z_at = spread(where_z, at + 3, NZ).astype(BF16)
    lanes_z = lax.broadcasted_iota(jnp.int32, (NZ, 128), 0).astype(F32).astype(BF16)
    hot = jnp.where(lanes_z == z_at, jnp.ones((), BF16), jnp.zeros((), BF16))
    plane = spread(plane, at + 3)
    at_x = lax.shift_right_arithmetic(plane, 3)
    at_y = plane & 7
    f = spread(tile, at)
    g = spread(tile, at + 1)
    h = spread(tile, at + 2)
    row = lax.broadcasted_iota(jnp.int32, (8, 128), 0)
    zero = jnp.zeros((8, 128), F32)
    weight_y = jnp.where(row == at_y, 1.0 - g, jnp.where(row == at_y + 1, g, zero))
    last_y = jnp.where(at_y == BY - 1, g, zero)
    weight_x = jnp.where(row == at_x, 1.0 - f, jnp.where(row == at_x + 1, f, zero))
    planes = []
    for i in range(BX + 1):
        here = jnp.where(at_x == i, 1.0 - f, jnp.where(at_x == i - 1, f, zero))
        planes.append(here * weight_y)
    planes.insert(2, weight_x * last_y)
    both = jnp.concatenate(planes, 0)
    tall = jnp.broadcast_to(h[:1], (48, 128))
    upper = both * tall
    lower = both - upper
    joint = jnp.concatenate([lower, upper], 0)
    high = joint.astype(BF16)
    low = (joint - high.astype(F32)).astype(BF16)
    return hot, jnp.concatenate([high, low], 0)


def body(
    cells_hbm, offsets_hbm, counts, ct_hbm, w_first, w_mid_in, w_last_in, w_head_in,
    force, sums,
    cells, offsets, ct_own, ct_in, force_s,
    packed, got, hot_s, wt_s, dep, dep_in, dens_f, dens, one, two, g_three, g_two, pre_one, pre_two, acc,
    base, w_one, w_mid, w_last, w_mid_t, w_last_t, head_f, head_b, ct_s,
    pay, half_in, ring, tile, tile_in, tiles,
    load, send, recv, send_d, recv_d, send_s, recv_s, send_p, recv_p, send_f, recv_f, send_m, recv_m,
):
    n_slab, n_sub = lax.axis_size("slab"), lax.axis_size("sub")
    slab, sub = lax.axis_index("slab"), lax.axis_index("sub")
    devices = n_slab * n_sub
    me = slab * n_sub + sub
    other = (sub + 1) % n_sub
    stop = ring_stop(slab)
    up, down = ring_slab((stop + 1) % n_slab), ring_slab((stop + n_slab - 1) % n_slab)
    neighbours = ((up, sub), (down, sub), (slab, other), (up, other), (down, other))
    worker, owner = (ring_slab(slab), other), (stop, other)
    axes = []
    for stride in (1, 4, 16):
        size = min(4, max(1, n_slab // stride))
        at = slab // stride % size
        axes.append((at, [slab + ((at + i) % size - at) * stride for i in range(1, size)]))

    loads = [
        pltpu.make_async_copy(src, dst, load.at[at])
        for at, (src, dst) in enumerate(
            ((cells_hbm.at[0], cells), (offsets_hbm.at[0], offsets), (ct_hbm, ct_own))
        )
    ]
    for copy in loads:
        copy.start()

    def partner(turn):
        to = (me + turn) % devices
        return (to // n_sub, to % n_sub), ring_stop(to // n_sub) * n_sub + (to + 1) % n_sub

    barrier = pltpu.get_barrier_semaphore()

    def greet(turn, carry):
        pl.semaphore_signal(barrier, inc=1, device_id=partner(turn)[0], device_id_type=MESH)
        return carry

    lax.fori_loop(1, devices, greet, 0)
    make_tables(w_first, w_mid_in, w_last_in, w_head_in, base, w_one, w_mid, w_last, w_mid_t,
                w_last_t, head_f, head_b)
    for copy in loads:
        copy.wait()

    diagonal = lax.broadcasted_iota(jnp.int32, (devices, devices), 0) == lax.broadcasted_iota(
        jnp.int32, (devices, devices), 1
    )
    used = jnp.broadcast_to(counts[...].astype(F32), (devices, devices))
    used = jnp.sum(jnp.where(diagonal, used, 0.0), 1, keepdims=True)
    slot = lax.broadcasted_iota(jnp.int32, (devices, 256), 1).astype(F32)
    live = jnp.where(slot < used, cells[...].astype(F32), -1.0)
    for first in range(0, devices, 8):
        some = slice(first, first + 8)
        for half in range(2):
            lanes = slice(half * 128, half * 128 + 128)
            for part in range(4):
                rows = pl.ds(first * 8 + 4 * half + part, 8, stride=8)
                packed[rows, :] = offsets[part, some, lanes] if part < 3 else live[some, lanes]

    def remote(src, dst, at, device, sends, recvs):
        return pltpu.make_async_remote_copy(
            src_ref=src, dst_ref=dst, send_sem=sends.at[at], recv_sem=recvs.at[at],
            device_id=device, device_id_type=MESH,
        )

    pl.semaphore_wait(barrier, devices - 1)

    def tile_rows(at):
        return pl.ds(pl.multiple_of(at * 8, 8), 8)

    def send_tile(turn, carry):
        device, brick = partner(turn)
        remote(
            packed.at[tile_rows(brick)], got.at[tile_rows(turn)], turn // (2 * GROUP), device,
            send_p, recv_p,
        ).start()
        return carry

    lax.fori_loop(1, devices, send_tile, 0)
    got[:8] = packed[tile_rows(partner(0)[1])]
    ct_copy = remote(ct_own, ct_in, 0, worker, send_f, recv_f)
    ct_copy.start()

    def arrived(step, tiles_in):
        rows = pl.ds(0, tiles_in * 8)
        return pltpu.make_async_copy(got.at[rows], got.at[rows], recv_p.at[step])

    def left(step, tiles_out):
        rows = pl.ds(0, tiles_out * 8)
        return pltpu.make_async_copy(packed.at[rows], packed.at[rows], send_p.at[step])

    def gather(step, total):
        for part in range(2):
            for k in range(GROUP):
                source = got[tile_rows(step * 2 * GROUP + part * GROUP + k)]
                for half in range(2):
                    hot, weights = source_terms(source, half)
                    at = k * 256 + half * 128
                    hot_s[part, :, at : at + 128] = hot
                    wt_s[part, :, at : at + 128] = weights
            result = dot_nt(wt_s[part], hot_s[part])
            total = total + result[:96] + result[96:]
        return total

    def wait_and_gather(step, total):
        arrived(step, 2 * GROUP).wait()
        return gather(step, total)

    arrived(0, 2 * GROUP - 1).wait()
    dep2 = gather(0, jnp.zeros((96, NZ), F32))
    dep2 = lax.fori_loop(1, devices // (2 * GROUP), wait_and_gather, dep2)
    dep[...] = dep2[:48] + lane_roll(dep2[48:], 1)
    left(0, 2 * GROUP - 1).wait()

    def sent(step, carry):
        left(step, 2 * GROUP).wait()
        return carry

    lax.fori_loop(1, devices // (2 * GROUP), sent, 0)

    upper_rows, lower_rows = pl.ds(16, 32), pl.ds(0, 24)
    copies = []
    for at, (device, rows) in enumerate(
        zip(neighbours, (upper_rows, lower_rows, pl.ds(0, 48), upper_rows, lower_rows))
    ):
        copies.append(remote(dep.at[rows], dep_in.at[at, rows], at, device, send_d, recv_d))
    for copy in copies:
        copy.start()

    dens_f[...] = jnp.zeros_like(dens_f)

    def place(source, source_x, x):
        base = (x + 2) * 16
        dens_f[base + 2 : base + 10] += source[X_ROW[source_x] : X_ROW[source_x] + 8]
        dens_f[base + 10 : base + 11] += source[16 + source_x : 17 + source_x]

    def place_other(source, source_x, x):
        base, row = (x + 2) * 16, X_ROW[source_x]
        dens_f[base : base + 2] += source[row + 6 : row + 8]
        dens_f[base + 2 : base + 3] += source[16 + source_x : 17 + source_x]
        dens_f[base + 10 : base + 12] += source[row : row + 2]

    for x in range(BX + 1):
        place(dep, x, x)
    for copy in copies:
        copy.wait()
    for x in (2, 3, 4):
        place(dep_in.at[0], x, x - 4)
    for x in (0, 1):
        place(dep_in.at[1], x, x + 4)
    for x in range(BX + 1):
        place_other(dep_in.at[2], x, x)
    for x in (2, 3, 4):
        place_other(dep_in.at[3], x, x - 4)
    for x in (0, 1):
        place_other(dep_in.at[4], x, x + 4)
    dens[...] = dens_f[...].astype(BF16)

    for y in range(BY + 2):
        taps = lane_roll(w_one[...], y).astype(BF16)
        pre = join_z(dot(taps, dens[...]))
        one[y] = (pre * sigmoid(pre)).astype(BF16)
        if 1 <= y <= BY:
            pre_one[y - 1] = pre[CORE]

    right, left_end = pl.ds(BX * CH, CH), pl.ds(CH, CH)
    before, after = pl.ds(0, CH), pl.ds((BX + 1) * CH, CH)
    core = pl.ds(CH, BX * CH)

    def rims(field, base, part):
        ys = pl.ds(1 + part * (BY // 2), BY // 2)
        edge, to = (1, BY + 1) if part == 0 else (BY, 0)
        plan = (
            ((slab, other), (edge, core), (to, core)),
            ((up, other), (edge, right), (to, before)),
            ((down, other), (edge, left_end), (to, after)),
            ((up, sub), (ys, right), (ys, before)),
            ((down, sub), (ys, left_end), (ys, after)),
        )
        started = []
        for at, (device, src, dst) in enumerate(plan):
            place = base + part * len(plan) + at
            copy = remote(field.at[src], field.at[dst], place, device, send, recv)
            copy.start()
            started.append(copy)
        return started

    def planes(field, y):
        return field[y : y + 3].reshape(3 * COLS, NZ)

    def conv(taps, field, y):
        return join_z(dot(taps[...], planes(field, y)))

    started = []
    for y in range(BY):
        pre = conv(w_mid, one, y)
        pre_two[y] = pre
        two[y + 1, CORE] = (pre * sigmoid(pre)).astype(BF16)
        if y % 4 == 3:
            started += rims(two, 0, y // 4)
    ct_copy.wait()
    ct_s[...] = jnp.zeros_like(ct_s)
    for k in range(3):
        for x in range(BX):
            at = (k * BX + x) * BY
            ct_s[at : at + BY] = ct_in[k, x]
    for copy in started:
        copy.wait()

    row_y = lax.broadcasted_iota(jnp.int32, (128, 128), 0) % BY
    lane_y = lax.broadcasted_iota(jnp.int32, (128, 128), 1) % BY
    out = jnp.zeros((96, NZ), F32)
    head = jnp.zeros((128, 128), F32)
    started = []
    for y in range(BY):
        pre = conv(w_last, two, y)
        s = sigmoid(pre)
        features = jnp.concatenate([(pre * s).astype(BF16), one[y + 1, CORE]], 0)
        taps = jnp.where(row_y == y, head_f[...], 0.0)[:96].astype(BF16)
        out = out + dot(taps, features)
        head = head + jnp.where(row_y == y, dot_nt(ct_s[...], features), 0.0)
        taps = jnp.where(lane_y == y, head_b[...], 0.0)[: BX * CH].astype(BF16)
        back = dot(taps, ct_s[...])
        g_three[y + 1, CORE] = (back * (s * (1.0 + pre * (1.0 - s)))).astype(BF16)
        if y % 4 == 3:
            started += rims(g_three, 10, y // 4)
    for k in range(3):
        for x in range(BX):
            at = (k * BX + x) * BY
            force_s[k, x] = out[at : at + BY].astype(BF16)
    force_copy = remote(force_s, force, 1, owner, send_f, recv_f)
    force_copy.start()

    def weight_grad(grads, field, out):
        acc[:, 3 * COLS :] = jnp.zeros((192, 96), F32)
        for y in range(BY):
            term = dot_nt(spread_z(grads[y + 1, CORE].astype(F32)), planes(field, y))
            if y == 0:
                acc[:, : 3 * COLS] = term
            else:
                acc[:, : 3 * COLS] += term
        rows = []
        for dz in range(3):
            total = jnp.zeros((CH, 384), F32)
            for x in range(BX):
                at = (dz * BX + x) * CH
                total = total + lane_roll(acc[at : at + CH], -CH * x)
            rows.append(total)
        joint = jnp.concatenate(rows, 0)
        lane = lax.broadcasted_iota(jnp.int32, joint.shape, 1)
        joint = jnp.where((lane % 96 < 48) & (lane < 3 * COLS), joint, 0.0)
        moved = [jnp.where(lane < 48, joint, 0.0)]
        for dy in (1, 2):
            inside = (lane >= 48 * dy) & (lane < 48 * dy + 48)
            moved.append(jnp.where(inside, lane_roll(joint, -48 * dy), 0.0))
        joint = moved[0] + moved[1] + moved[2]
        out[:48] = joint[:, :128]
        tail = joint[:CH, 128:256]
        for dz in (1, 2):
            tail = tail + lane_roll(joint[dz * CH : dz * CH + CH, 128:256], dz * CH)
        out[48:] = tail

    theirs = pl.ds(pl.multiple_of(other * 32, 8), 32)
    mine = pl.ds(pl.multiple_of(sub * 32, 8), 32)

    class Sum:
        def __init__(self, at):
            self.at, self.next, self.copies = at, at * 38, []

        def begin(self, src, dst, device):
            self.copies.append(remote(src, dst, self.next, device, send_s, recv_s))
            self.copies[-1].start()
            self.next += 1

        def end(self):
            for copy in self.copies:
                copy.wait()
            self.copies = []

        def across(self):
            self.begin(pay.at[self.at, theirs], half_in.at[self.at], (slab, other))

        def joined(self):
            self.end()
            return pay[self.at, mine] + half_in[self.at]

        def out(self, turn, total):
            for part in range(4):
                at, peers = axes[(part + turn) % 3]
                rows = pl.ds(part * 8, 8)
                ring[self.at, turn, at, rows] = total[part * 8 : part * 8 + 8]
                for peer in peers:
                    slot = ring.at[self.at, turn, at, rows]
                    self.begin(slot, slot, (peer, sub))

        def back(self, turn):
            self.end()
            parts = []
            for part in range(4):
                rows = slice(part * 8, part * 8 + 8)
                value = ring[self.at, turn, 0, rows]
                for slot in range(1, len(axes[(part + turn) % 3][1]) + 1):
                    value = value + ring[self.at, turn, slot, rows]
                parts.append(value)
            return jnp.concatenate(parts, 0)

        def share(self, total):
            rows = pl.ds(pl.multiple_of(self.at * 64 + sub * 32, 8), 32)
            sums[rows] = total * scale
            self.begin(sums.at[rows], sums.at[rows], (slab, other))

    scale = 1.0 / math.sqrt(BX * n_slab * BY * n_sub * NZ)
    sum_last, sum_mid = Sum(0), Sum(1)

    weight_grad(g_three, two, pay.at[0])
    row = lax.broadcasted_iota(jnp.int32, (128, 128), 0)
    lane = lax.broadcasted_iota(jnp.int32, (128, 128), 1)
    head = jnp.where(lane % 64 // CH == row // BY % BX, head, 0.0)
    kept = jnp.concatenate(
        [jnp.sum(head[k * 32 : k * 32 + 32], 0, keepdims=True) for k in range(3)]
        + [jnp.zeros((5, 128), F32)],
        0,
    )
    kept = kept + lane_roll(kept, -2 * CH)
    kept = kept + lane_roll(kept, -CH)
    lane = lax.broadcasted_iota(jnp.int32, (8, 128), 1)
    top = jnp.where(lane < CH, kept, 0.0) + jnp.where(
        (lane >= CH) & (lane < 2 * CH), lane_roll(kept, -48), 0.0
    )
    pay[0, 48:56] += lane_roll(top, 48)
    sum_last.across()
    for copy in started:
        copy.wait()

    started = []
    for y in range(BY):
        back = conv(w_last_t, g_three, y)
        g_two[y + 1, CORE] = (back * slope(pre_two[y])).astype(BF16)
        if y % 4 == 3:
            started += rims(g_two, 20, y // 4)
    sum_last.out(0, sum_last.joined())
    weight_grad(g_two, one, pay.at[1])
    sum_mid.across()
    sum_last.out(1, sum_last.back(0))
    for copy in started:
        copy.wait()
    sum_mid.out(0, sum_mid.joined())

    first = jnp.zeros((192, 128), F32)
    for y in range(BY):
        taps = jnp.where(lane_y == y, head_b[...], 0.0)[BX * CH :].astype(BF16)
        back = conv(w_mid_t, g_two, y) + dot(taps, ct_s[...])
        grad = (back * slope(pre_one[y])).astype(BF16).astype(F32)
        first = first + lane_roll(dot_nt(spread_z(grad), dens[...]), -y)
    rows = []
    for dz in range(3):
        total = jnp.zeros((CH, 128), F32)
        for x in range(BX):
            at = (dz * BX + x) * CH
            total = total + lane_roll(first[at : at + CH], -(16 * x + 17))
        rows.append(total)
    joint = jnp.concatenate(rows, 0)
    lane = lax.broadcasted_iota(jnp.int32, joint.shape, 1)
    joint = jnp.where((lane % 16 < 3) & (lane < 48), joint, 0.0)
    value = jnp.zeros((8, 128), F32)
    for block, shift in enumerate(BLOCK_LANE):
        value = value + lane_roll(joint[block * 8 : block * 8 + 8], shift)
    tile[...] = value
    tile_copy = remote(tile, tile_in, 2, (slab, other), send_f, recv_f)
    tile_copy.start()
    sum_mid.out(1, sum_mid.back(0))
    sum_last.out(2, sum_last.back(1))
    tile_copy.wait()
    tiles[slab] = tile[...] + tile_in[...]
    if n_slab > 1:

        def spread_tile(turn, carry):
            peer = (slab + 1 + (turn + n_slab * 2 // 3) % (n_slab - 1)) % n_slab
            remote(tiles.at[slab], tiles.at[slab], 0, (peer, sub), send_m, recv_m).start()
            return carry

        lax.fori_loop(0, n_slab - 1, spread_tile, 0)
    sum_mid.out(2, sum_mid.back(1))
    sum_last.share(sum_last.back(2))
    sum_mid.share(sum_mid.back(2))
    if n_slab > 1:
        some = pl.ds(0, n_slab - 1)
        pltpu.make_async_copy(tiles.at[some], tiles.at[some], recv_m.at[0]).wait()
        pltpu.make_async_copy(tiles.at[some], tiles.at[some], send_m.at[0]).wait()
    sums[128:136] = jnp.sum(tiles[...], 0) * scale
    sum_last.end()
    sum_mid.end()
    force_copy.wait()


def ring_stop(slab):
    y = (slab // 4 + slab // 16) % 4
    return slab // 16 * 16 + y * 4 + (slab + y) % 4


def ring_slab(stop):
    z, y = stop // 16, stop // 4 % 4
    return z * 16 + (y + 4 - z) % 4 * 4 + (stop + 4 - y) % 4


def finish(force_in, sums, force, grad_first, grad_mid, grad_last, grad_head):
    force[...] = force_in[...]
    for dx, dy, dz in OFFSETS:
        tap, rows, at = dx * 9 + dy * 3 + dz, dz * CH, dy * 48 + dx * CH
        if at == 128:
            rows, at = 48, dz * CH
        for first, out in ((64, grad_mid), (0, grad_last)):
            block = sums[first + rows : first + rows + CH, at : at + CH]
            out[:, tap * CH : tap * CH + CH] = block
        for half in range(2):
            at = BLOCK_LANE[2 * dz + half] + dx * CH + dy
            grad_first[half * 8 : half * 8 + 8, tap : tap + 1] = sums[128:136, at : at + 1]
    grad_head[...] = sums[48:51, 48:80]


BLOCK_LANE = (0, 3, 6, 9, 12, 48)
OFFSETS = [(dx, dy, dz) for dx in range(3) for dy in range(3) for dz in range(3)]


def make_tables(w_first, w_mid, w_last, w_head, base, one, mid, last, mid_t, last_t, head_f, head_b):
    def spread(out):
        for dz in range(3):
            for x in range(BX):
                at = (dz * BX + x) * CH
                moved = lane_roll(base[dz * CH : dz * CH + CH], x * CH)
                out[at : at + CH] = moved[:, : 3 * COLS].astype(BF16)

    base[...] = jnp.zeros_like(base)
    for source, out, out_t in ((w_mid, mid, mid_t), (w_last, last, last_t)):
        weights = source[...].astype(F32)
        for dx, dy, dz in OFFSETS:
            tap, at = dx * 9 + dy * 3 + dz, dy * 96 + dx * CH
            base[dz * CH : dz * CH + CH, at : at + CH] = weights[:, tap * CH : tap * CH + CH]
        spread(out)
        padded = jnp.concatenate([weights, jnp.zeros((CH, 80), F32)], 1)
        turned = jnp.concatenate([padded, jnp.zeros((112, 512), F32)], 0).T
        for dx, dy, dz in OFFSETS:
            tap, at = dx * 9 + dy * 3 + dz, (2 - dy) * 96 + (2 - dx) * CH
            to = (2 - dz) * CH
            base[to : to + CH, at : at + CH] = turned[tap * CH : tap * CH + CH, :CH]
        spread(out_t)
    base[...] = jnp.zeros_like(base)
    weights = w_first[...].astype(F32)
    for dx, dy, dz in OFFSETS:
        tap, at = dx * 9 + dy * 3 + dz, dx * 16 + dy
        base[dz * CH : dz * CH + CH, at : at + 1] = weights[:, tap : tap + 1]
    for dz in range(3):
        for x in range(BX + 2):
            at = (dz * (BX + 2) + x) * CH
            one[at : at + CH] = lane_roll(base[dz * CH : dz * CH + CH, :128], x * 16)
    head_f[...] = jnp.zeros_like(head_f)
    weights = w_head[...].astype(F32)
    for k in range(3):
        for x in range(BX):
            at = (k * BX + x) * BY
            for half in range(2):
                row = weights[k : k + 1, half * CH : half * CH + CH]
                to = half * 64 + x * CH
                head_f[at : at + BY, to : to + CH] = jnp.broadcast_to(row, (BY, CH))
    head_b[...] = head_f[...].T


def per_device(part_cells, part_offsets, part_counts, w_first, w_mid, w_last, w_head, cotangent):
    devices = part_counts.shape[1]
    vmem = pl.BlockSpec(memory_space=pltpu.VMEM)
    field = pltpu.VMEM((BY + 2, COLS, NZ), BF16)
    kept = pltpu.VMEM((BY, BX * CH, NZ), F32)
    table = pltpu.VMEM((192, 3 * COLS), BF16)
    hbm = pl.BlockSpec(memory_space=pltpu.HBM)
    slots = part_cells.shape[2]
    force, sums = pl.pallas_call(
        body,
        out_shape=(
            jax.ShapeDtypeStruct(cotangent.shape, BF16),
            jax.ShapeDtypeStruct((136, 128), F32),
        ),
        in_specs=[hbm, hbm, vmem, hbm, vmem, vmem, vmem, vmem],
        out_specs=[vmem] * 2,
        scratch_shapes=[
            pltpu.VMEM((devices, slots), jnp.int32),
            pltpu.VMEM((3, devices, slots), F32),
            pltpu.VMEM(cotangent.shape, BF16),
            pltpu.VMEM(cotangent.shape, BF16),
            pltpu.VMEM(cotangent.shape, BF16),
            pltpu.VMEM((devices * 8, 128), F32),
            pltpu.VMEM((devices * 8, 128), F32),
            pltpu.VMEM((2, NZ, 256 * GROUP), BF16),
            pltpu.VMEM((2, 192, 256 * GROUP), BF16),
            pltpu.VMEM((48, NZ), F32),
            pltpu.VMEM((5, 48, NZ), F32),
            pltpu.VMEM((128, NZ), F32),
            pltpu.VMEM((128, NZ), BF16),
            field, field, field, field, kept, kept,
            pltpu.VMEM((192, 384), F32),
            pltpu.VMEM((48, 384), F32),
            pltpu.VMEM((288, 128), F32),
            table, table, table, table,
            pltpu.VMEM((128, 128), F32),
            pltpu.VMEM((128, 128), F32),
            pltpu.VMEM((128, NZ), BF16),
            pltpu.VMEM((2, 64, 128), F32),
            pltpu.VMEM((2, 32, 128), F32),
            pltpu.VMEM((2, 3, 4, 32, 128), F32),
            pltpu.VMEM((8, 128), F32),
            pltpu.VMEM((8, 128), F32),
            pltpu.VMEM((devices // 2, 8, 128), F32),
            pltpu.SemaphoreType.DMA((3,)),
            pltpu.SemaphoreType.DMA((30,)),
            pltpu.SemaphoreType.DMA((30,)),
            pltpu.SemaphoreType.DMA((5,)),
            pltpu.SemaphoreType.DMA((5,)),
            pltpu.SemaphoreType.DMA((76,)),
            pltpu.SemaphoreType.DMA((76,)),
            pltpu.SemaphoreType.DMA((devices // (2 * GROUP),)),
            pltpu.SemaphoreType.DMA((devices // (2 * GROUP),)),
            pltpu.SemaphoreType.DMA((3,)),
            pltpu.SemaphoreType.DMA((3,)),
            pltpu.SemaphoreType.DMA((1,)),
            pltpu.SemaphoreType.DMA((1,)),
        ],
        compiler_params=pltpu.CompilerParams(
            collective_id=0, has_side_effects=True, vmem_limit_bytes=60 << 20
        ),
        name="level",
    )(part_cells, part_offsets.transpose(0, 2, 1, 3), part_counts, cotangent, w_first, w_mid, w_last, w_head)
    return pl.pallas_call(
        finish,
        out_shape=(
            jax.ShapeDtypeStruct(cotangent.shape, BF16),
            jax.ShapeDtypeStruct(w_first.shape, F32),
            jax.ShapeDtypeStruct(w_mid.shape, F32),
            jax.ShapeDtypeStruct(w_last.shape, F32),
            jax.ShapeDtypeStruct(w_head.shape, F32),
        ),
        in_specs=[vmem] * 2,
        out_specs=[vmem] * 5,
        compiler_params=pltpu.CompilerParams(vmem_limit_bytes=60 << 20),
        name="finish",
    )(force, sums)


def solution(mesh):
    in_specs = (
        P(("slab", "sub"), None, None),
        P(("slab", "sub"), None, None, None),
        P(("slab", "sub"), None),
        P(), P(), P(), P(),
        P(None, "slab", "sub", None),
    )
    out_specs = (P(None, "slab", "sub", None), P(), P(), P(), P())
    return jax.shard_map(
        per_device, mesh=mesh, in_specs=in_specs, out_specs=out_specs, check_vma=False
    )
```

```python
import functools
import math

import jax
import jax.numpy as jnp
from jax import lax
from jax.experimental import pallas as pl
from jax.experimental.pallas import tpu as pltpu
from jax.sharding import PartitionSpec as P

MESH = pl.DeviceIdType.MESH
F32 = jnp.float32
BF16 = jnp.bfloat16

BX, BY, NZ, CH = 4, 8, 256, 16
COLS = (BX + 2) * CH
CORE = slice(CH, CH + BX * CH)
GROUP = 4
X_ROW = (0, 8, 24, 32, 40)


def lane_roll(value, shift):
    return pltpu.roll(value, shift % value.shape[1], 1)


def dot(a, b):
    return jnp.dot(a, b, preferred_element_type=F32)


def dot_nt(a, b):
    return lax.dot_general(a, b, (((1,), (1,)), ((), ())), preferred_element_type=F32)


def join_z(stacked):
    rows = stacked.shape[0] // 3
    below = lane_roll(stacked[:rows], 1)
    above = lane_roll(stacked[2 * rows :], -1)
    return stacked[rows : 2 * rows] + below + above


def spread_z(grad):
    return jnp.concatenate([lane_roll(grad, -1), grad, lane_roll(grad, 1)], 0).astype(BF16)


def sigmoid(value):
    return 1.0 / (1.0 + jnp.exp(-value))


def slope(value):
    s = sigmoid(value)
    return s * (1.0 + value * (1.0 - s))


def source_terms(tile, half):
    cell = tile.astype(jnp.int32)
    where_z = jnp.where(cell < 0, -1, cell & 255).astype(F32)
    plane = lax.shift_right_arithmetic(cell, 8)

    def spread(value, row, rows=8):
        return jnp.broadcast_to(value[row : row + 1], (rows, 128))

    at = 4 * half
    z_at = spread(where_z, at + 3, NZ).astype(BF16)
    lanes_z = lax.broadcasted_iota(jnp.int32, (NZ, 128), 0).astype(F32).astype(BF16)
    hot = jnp.where(lanes_z == z_at, jnp.ones((), BF16), jnp.zeros((), BF16))
    plane = spread(plane, at + 3)
    at_x = lax.shift_right_arithmetic(plane, 3)
    at_y = plane & 7
    f = spread(tile, at)
    g = spread(tile, at + 1)
    h = spread(tile, at + 2)
    row = lax.broadcasted_iota(jnp.int32, (8, 128), 0)
    zero = jnp.zeros((8, 128), F32)
    weight_y = jnp.where(row == at_y, 1.0 - g, jnp.where(row == at_y + 1, g, zero))
    last_y = jnp.where(at_y == BY - 1, g, zero)
    weight_x = jnp.where(row == at_x, 1.0 - f, jnp.where(row == at_x + 1, f, zero))
    planes = []
    for i in range(BX + 1):
        here = jnp.where(at_x == i, 1.0 - f, jnp.where(at_x == i - 1, f, zero))
        planes.append(here * weight_y)
    planes.insert(2, weight_x * last_y)
    both = jnp.concatenate(planes, 0)
    tall = jnp.broadcast_to(h[:1], (48, 128))
    upper = both * tall
    lower = both - upper
    joint = jnp.concatenate([lower, upper], 0)
    high = joint.astype(BF16)
    low = (joint - high.astype(F32)).astype(BF16)
    return hot, jnp.concatenate([high, low], 0)


def body(
    cells_hbm, offsets_hbm, counts, ct_hbm, w_first, w_mid_in, w_last_in, w_head_in,
    force, sums,
    cells, offsets, ct_own, ct_in, force_s,
    packed, got, hot_s, wt_s, dep, dep_in, dens_f, dens, one, two, g_three, g_two, pre_one, pre_two, acc,
    base, w_one, w_mid, w_last, w_mid_t, w_last_t, head_f, head_b, ct_s,
    pay, half_in, ring, tile, tile_in, tiles,
    load, send, recv, send_d, recv_d, send_s, recv_s, send_p, recv_p, send_f, recv_f, send_m, recv_m,
):
    n_slab, n_sub = lax.axis_size("slab"), lax.axis_size("sub")
    slab, sub = lax.axis_index("slab"), lax.axis_index("sub")
    devices = n_slab * n_sub
    me = slab * n_sub + sub
    other = (sub + 1) % n_sub
    stop = ring_stop(slab)
    up, down = ring_slab((stop + 1) % n_slab), ring_slab((stop + n_slab - 1) % n_slab)
    neighbours = ((up, sub), (down, sub), (slab, other), (up, other), (down, other))
    worker, owner = (ring_slab(slab), other), (stop, other)
    axes = []
    for stride in (1, 4, 16):
        size = min(4, max(1, n_slab // stride))
        at = slab // stride % size
        axes.append((at, [slab + ((at + i) % size - at) * stride for i in range(1, size)]))

    loads = [
        pltpu.make_async_copy(src, dst, load.at[at])
        for at, (src, dst) in enumerate(
            ((cells_hbm.at[0], cells), (offsets_hbm.at[0], offsets), (ct_hbm, ct_own))
        )
    ]
    for copy in loads:
        copy.start()

    def partner(turn):
        to = (me + turn) % devices
        return (to // n_sub, to % n_sub), ring_stop(to // n_sub) * n_sub + (to + 1) % n_sub

    barrier = pltpu.get_barrier_semaphore()

    def greet(turn, carry):
        pl.semaphore_signal(barrier, inc=1, device_id=partner(turn)[0], device_id_type=MESH)
        return carry

    lax.fori_loop(1, devices, greet, 0)
    make_tables(w_first, w_mid_in, w_last_in, w_head_in, base, w_one, w_mid, w_last, w_mid_t,
                w_last_t, head_f, head_b)
    for copy in loads:
        copy.wait()

    diagonal = lax.broadcasted_iota(jnp.int32, (devices, devices), 0) == lax.broadcasted_iota(
        jnp.int32, (devices, devices), 1
    )
    used = jnp.broadcast_to(counts[...].astype(F32), (devices, devices))
    used = jnp.sum(jnp.where(diagonal, used, 0.0), 1, keepdims=True)
    slot = lax.broadcasted_iota(jnp.int32, (devices, 256), 1).astype(F32)
    live = jnp.where(slot < used, cells[...].astype(F32), -1.0)
    for first in range(0, devices, 8):
        some = slice(first, first + 8)
        for half in range(2):
            lanes = slice(half * 128, half * 128 + 128)
            for part in range(4):
                rows = pl.ds(first * 8 + 4 * half + part, 8, stride=8)
                packed[rows, :] = offsets[part, some, lanes] if part < 3 else live[some, lanes]

    def remote(src, dst, at, device, sends, recvs):
        return pltpu.make_async_remote_copy(
            src_ref=src, dst_ref=dst, send_sem=sends.at[at], recv_sem=recvs.at[at],
            device_id=device, device_id_type=MESH,
        )

    pl.semaphore_wait(barrier, devices - 1)

    def tile_rows(at):
        return pl.ds(pl.multiple_of(at * 8, 8), 8)

    def send_tile(turn, carry):
        device, brick = partner(turn)
        remote(
            packed.at[tile_rows(brick)], got.at[tile_rows(turn)], turn // (2 * GROUP), device,
            send_p, recv_p,
        ).start()
        return carry

    lax.fori_loop(1, devices, send_tile, 0)
    got[:8] = packed[tile_rows(partner(0)[1])]
    ct_copy = remote(ct_own, ct_in, 0, worker, send_f, recv_f)
    ct_copy.start()

    def arrived(step, tiles_in):
        rows = pl.ds(0, tiles_in * 8)
        return pltpu.make_async_copy(got.at[rows], got.at[rows], recv_p.at[step])

    def left(step, tiles_out):
        rows = pl.ds(0, tiles_out * 8)
        return pltpu.make_async_copy(packed.at[rows], packed.at[rows], send_p.at[step])

    def build(step, part):
        for k in range(GROUP):
            source = got[tile_rows(step * 2 * GROUP + part * GROUP + k)]
            for half in range(2):
                hot, weights = source_terms(source, half)
                at = k * 256 + half * 128
                hot_s[part, :, at : at + 128] = hot
                wt_s[part, :, at : at + 128] = weights

    def product(part):
        result = dot_nt(wt_s[part], hot_s[part])
        return result[:96] + result[96:]

    def gather(step, total):
        total = total + product(0)
        build(step, 1)
        arrived(step + 1, 2 * GROUP).wait()
        total = total + product(1)
        build(step + 1, 0)
        return total

    steps = devices // (2 * GROUP)
    arrived(0, 2 * GROUP - 1).wait()
    build(0, 0)
    dep2 = lax.fori_loop(0, steps - 1, gather, jnp.zeros((96, NZ), F32))
    dep2 = dep2 + product(0)
    build(steps - 1, 1)
    dep2 = dep2 + product(1)
    dep[...] = dep2[:48] + lane_roll(dep2[48:], 1)
    left(0, 2 * GROUP - 1).wait()

    def sent(step, carry):
        left(step, 2 * GROUP).wait()
        return carry

    lax.fori_loop(1, devices // (2 * GROUP), sent, 0)

    upper_rows, lower_rows = pl.ds(16, 32), pl.ds(0, 24)
    copies = []
    for at, (device, rows) in enumerate(
        zip(neighbours, (upper_rows, lower_rows, pl.ds(0, 48), upper_rows, lower_rows))
    ):
        copies.append(remote(dep.at[rows], dep_in.at[at, rows], at, device, send_d, recv_d))
    for copy in copies:
        copy.start()

    dens_f[...] = jnp.zeros_like(dens_f)

    def place(source, source_x, x):
        base = (x + 2) * 16
        dens_f[base + 2 : base + 10] += source[X_ROW[source_x] : X_ROW[source_x] + 8]
        dens_f[base + 10 : base + 11] += source[16 + source_x : 17 + source_x]

    def place_other(source, source_x, x):
        base, row = (x + 2) * 16, X_ROW[source_x]
        dens_f[base : base + 2] += source[row + 6 : row + 8]
        dens_f[base + 2 : base + 3] += source[16 + source_x : 17 + source_x]
        dens_f[base + 10 : base + 12] += source[row : row + 2]

    for x in range(BX + 1):
        place(dep, x, x)
    for copy in copies:
        copy.wait()
    for x in (2, 3, 4):
        place(dep_in.at[0], x, x - 4)
    for x in (0, 1):
        place(dep_in.at[1], x, x + 4)
    for x in range(BX + 1):
        place_other(dep_in.at[2], x, x)
    for x in (2, 3, 4):
        place_other(dep_in.at[3], x, x - 4)
    for x in (0, 1):
        place_other(dep_in.at[4], x, x + 4)
    dens[...] = dens_f[...].astype(BF16)

    for y in range(BY + 2):
        taps = lane_roll(w_one[...], y).astype(BF16)
        pre = join_z(dot(taps, dens[...]))
        one[y] = (pre * sigmoid(pre)).astype(BF16)
        if 1 <= y <= BY:
            pre_one[y - 1] = pre[CORE]

    right, left_end = pl.ds(BX * CH, CH), pl.ds(CH, CH)
    before, after = pl.ds(0, CH), pl.ds((BX + 1) * CH, CH)
    core = pl.ds(CH, BX * CH)

    def rims(field, base, part):
        ys = pl.ds(1 + part * (BY // 2), BY // 2)
        edge, to = (1, BY + 1) if part == 0 else (BY, 0)
        plan = (
            ((slab, other), (edge, core), (to, core)),
            ((up, other), (edge, right), (to, before)),
            ((down, other), (edge, left_end), (to, after)),
            ((up, sub), (ys, right), (ys, before)),
            ((down, sub), (ys, left_end), (ys, after)),
        )
        started = []
        for at, (device, src, dst) in enumerate(plan):
            place = base + part * len(plan) + at
            copy = remote(field.at[src], field.at[dst], place, device, send, recv)
            copy.start()
            started.append(copy)
        return started

    def planes(field, y):
        return field[y : y + 3].reshape(3 * COLS, NZ)

    def conv(taps, field, y):
        return join_z(dot(taps[...], planes(field, y)))

    started = []
    for y in range(BY):
        pre = conv(w_mid, one, y)
        pre_two[y] = pre
        two[y + 1, CORE] = (pre * sigmoid(pre)).astype(BF16)
        if y % 4 == 3:
            started += rims(two, 0, y // 4)
    ct_copy.wait()
    ct_s[...] = jnp.zeros_like(ct_s)
    for k in range(3):
        for x in range(BX):
            at = (k * BX + x) * BY
            ct_s[at : at + BY] = ct_in[k, x]
    for copy in started:
        copy.wait()

    row_y = lax.broadcasted_iota(jnp.int32, (128, 128), 0) % BY
    lane_y = lax.broadcasted_iota(jnp.int32, (128, 128), 1) % BY
    out = jnp.zeros((96, NZ), F32)
    head = jnp.zeros((128, 128), F32)
    started = []
    for y in range(BY):
        pre = conv(w_last, two, y)
        s = sigmoid(pre)
        features = jnp.concatenate([(pre * s).astype(BF16), one[y + 1, CORE]], 0)
        taps = jnp.where(row_y == y, head_f[...], 0.0)[:96].astype(BF16)
        out = out + dot(taps, features)
        head = head + jnp.where(row_y == y, dot_nt(ct_s[...], features), 0.0)
        taps = jnp.where(lane_y == y, head_b[...], 0.0)[: BX * CH].astype(BF16)
        back = dot(taps, ct_s[...])
        g_three[y + 1, CORE] = (back * (s * (1.0 + pre * (1.0 - s)))).astype(BF16)
        if y % 4 == 3:
            started += rims(g_three, 10, y // 4)
    for k in range(3):
        for x in range(BX):
            at = (k * BX + x) * BY
            force_s[k, x] = out[at : at + BY].astype(BF16)
    force_copy = remote(force_s, force, 1, owner, send_f, recv_f)
    force_copy.start()

    def weight_grad(grads, field, out):
        acc[:, 3 * COLS :] = jnp.zeros((192, 96), F32)
        for y in range(BY):
            term = dot_nt(spread_z(grads[y + 1, CORE].astype(F32)), planes(field, y))
            if y == 0:
                acc[:, : 3 * COLS] = term
            else:
                acc[:, : 3 * COLS] += term
        rows = []
        for dz in range(3):
            total = jnp.zeros((CH, 384), F32)
            for x in range(BX):
                at = (dz * BX + x) * CH
                total = total + lane_roll(acc[at : at + CH], -CH * x)
            rows.append(total)
        joint = jnp.concatenate(rows, 0)
        lane = lax.broadcasted_iota(jnp.int32, joint.shape, 1)
        joint = jnp.where((lane % 96 < 48) & (lane < 3 * COLS), joint, 0.0)
        moved = [jnp.where(lane < 48, joint, 0.0)]
        for dy in (1, 2):
            inside = (lane >= 48 * dy) & (lane < 48 * dy + 48)
            moved.append(jnp.where(inside, lane_roll(joint, -48 * dy), 0.0))
        joint = moved[0] + moved[1] + moved[2]
        out[:48] = joint[:, :128]
        tail = joint[:CH, 128:256]
        for dz in (1, 2):
            tail = tail + lane_roll(joint[dz * CH : dz * CH + CH, 128:256], dz * CH)
        out[48:] = tail

    theirs = pl.ds(pl.multiple_of(other * 32, 8), 32)
    mine = pl.ds(pl.multiple_of(sub * 32, 8), 32)

    class Sum:
        def __init__(self, at):
            self.at, self.next, self.copies = at, at * 38, []

        def begin(self, src, dst, device):
            self.copies.append(remote(src, dst, self.next, device, send_s, recv_s))
            self.copies[-1].start()
            self.next += 1

        def end(self):
            for copy in self.copies:
                copy.wait()
            self.copies = []

        def across(self):
            self.begin(pay.at[self.at, theirs], half_in.at[self.at], (slab, other))

        def joined(self):
            self.end()
            return pay[self.at, mine] + half_in[self.at]

        def out(self, turn, total):
            for part in range(4):
                at, peers = axes[(part + turn) % 3]
                rows = pl.ds(part * 8, 8)
                ring[self.at, turn, at, rows] = total[part * 8 : part * 8 + 8]
                for peer in peers:
                    slot = ring.at[self.at, turn, at, rows]
                    self.begin(slot, slot, (peer, sub))

        def back(self, turn):
            self.end()
            parts = []
            for part in range(4):
                rows = slice(part * 8, part * 8 + 8)
                value = ring[self.at, turn, 0, rows]
                for slot in range(1, len(axes[(part + turn) % 3][1]) + 1):
                    value = value + ring[self.at, turn, slot, rows]
                parts.append(value)
            return jnp.concatenate(parts, 0)

        def share(self, total):
            rows = pl.ds(pl.multiple_of(self.at * 64 + sub * 32, 8), 32)
            sums[rows] = total * scale
            self.begin(sums.at[rows], sums.at[rows], (slab, other))

    scale = 1.0 / math.sqrt(BX * n_slab * BY * n_sub * NZ)
    sum_last, sum_mid = Sum(0), Sum(1)

    weight_grad(g_three, two, pay.at[0])
    row = lax.broadcasted_iota(jnp.int32, (128, 128), 0)
    lane = lax.broadcasted_iota(jnp.int32, (128, 128), 1)
    head = jnp.where(lane % 64 // CH == row // BY % BX, head, 0.0)
    kept = jnp.concatenate(
        [jnp.sum(head[k * 32 : k * 32 + 32], 0, keepdims=True) for k in range(3)]
        + [jnp.zeros((5, 128), F32)],
        0,
    )
    kept = kept + lane_roll(kept, -2 * CH)
    kept = kept + lane_roll(kept, -CH)
    lane = lax.broadcasted_iota(jnp.int32, (8, 128), 1)
    top = jnp.where(lane < CH, kept, 0.0) + jnp.where(
        (lane >= CH) & (lane < 2 * CH), lane_roll(kept, -48), 0.0
    )
    pay[0, 48:56] += lane_roll(top, 48)
    sum_last.across()
    for copy in started:
        copy.wait()

    started = []
    for y in range(BY):
        back = conv(w_last_t, g_three, y)
        g_two[y + 1, CORE] = (back * slope(pre_two[y])).astype(BF16)
        if y % 4 == 3:
            started += rims(g_two, 20, y // 4)
    sum_last.out(0, sum_last.joined())
    weight_grad(g_two, one, pay.at[1])
    sum_mid.across()
    sum_last.out(1, sum_last.back(0))
    for copy in started:
        copy.wait()
    sum_mid.out(0, sum_mid.joined())

    first = jnp.zeros((192, 128), F32)
    for y in range(BY):
        taps = jnp.where(lane_y == y, head_b[...], 0.0)[BX * CH :].astype(BF16)
        back = conv(w_mid_t, g_two, y) + dot(taps, ct_s[...])
        grad = (back * slope(pre_one[y])).astype(BF16).astype(F32)
        first = first + lane_roll(dot_nt(spread_z(grad), dens[...]), -y)
    rows = []
    for dz in range(3):
        total = jnp.zeros((CH, 128), F32)
        for x in range(BX):
            at = (dz * BX + x) * CH
            total = total + lane_roll(first[at : at + CH], -(16 * x + 17))
        rows.append(total)
    joint = jnp.concatenate(rows, 0)
    lane = lax.broadcasted_iota(jnp.int32, joint.shape, 1)
    joint = jnp.where((lane % 16 < 3) & (lane < 48), joint, 0.0)
    value = jnp.zeros((8, 128), F32)
    for block, shift in enumerate(BLOCK_LANE):
        value = value + lane_roll(joint[block * 8 : block * 8 + 8], shift)
    tile[...] = value
    tile_copy = remote(tile, tile_in, 2, (slab, other), send_f, recv_f)
    tile_copy.start()
    sum_mid.out(1, sum_mid.back(0))
    sum_last.out(2, sum_last.back(1))
    tile_copy.wait()
    tiles[slab] = tile[...] + tile_in[...]
    if n_slab > 1:

        def spread_tile(turn, carry):
            peer = (slab + 1 + (turn + n_slab * 2 // 3) % (n_slab - 1)) % n_slab
            remote(tiles.at[slab], tiles.at[slab], 0, (peer, sub), send_m, recv_m).start()
            return carry

        lax.fori_loop(0, n_slab - 1, spread_tile, 0)
    sum_mid.out(2, sum_mid.back(1))
    sum_last.share(sum_last.back(2))
    sum_mid.share(sum_mid.back(2))
    if n_slab > 1:
        some = pl.ds(0, n_slab - 1)
        pltpu.make_async_copy(tiles.at[some], tiles.at[some], recv_m.at[0]).wait()
        pltpu.make_async_copy(tiles.at[some], tiles.at[some], send_m.at[0]).wait()
    sums[128:136] = jnp.sum(tiles[...], 0) * scale
    sum_last.end()
    sum_mid.end()
    force_copy.wait()


def ring_stop(slab):
    y = (slab // 4 + slab // 16) % 4
    return slab // 16 * 16 + y * 4 + (slab + y) % 4


def ring_slab(stop):
    z, y = stop // 16, stop // 4 % 4
    return z * 16 + (y + 4 - z) % 4 * 4 + (stop + 4 - y) % 4


def finish(force_in, sums, force, grad_first, grad_mid, grad_last, grad_head):
    force[...] = force_in[...]
    for dx, dy, dz in OFFSETS:
        tap, rows, at = dx * 9 + dy * 3 + dz, dz * CH, dy * 48 + dx * CH
        if at == 128:
            rows, at = 48, dz * CH
        for first, out in ((64, grad_mid), (0, grad_last)):
            block = sums[first + rows : first + rows + CH, at : at + CH]
            out[:, tap * CH : tap * CH + CH] = block
        for half in range(2):
            at = BLOCK_LANE[2 * dz + half] + dx * CH + dy
            grad_first[half * 8 : half * 8 + 8, tap : tap + 1] = sums[128:136, at : at + 1]
    grad_head[...] = sums[48:51, 48:80]


BLOCK_LANE = (0, 3, 6, 9, 12, 48)
OFFSETS = [(dx, dy, dz) for dx in range(3) for dy in range(3) for dz in range(3)]


def make_tables(w_first, w_mid, w_last, w_head, base, one, mid, last, mid_t, last_t, head_f, head_b):
    def spread(out):
        for dz in range(3):
            for x in range(BX):
                at = (dz * BX + x) * CH
                moved = lane_roll(base[dz * CH : dz * CH + CH], x * CH)
                out[at : at + CH] = moved[:, : 3 * COLS].astype(BF16)

    base[...] = jnp.zeros_like(base)
    for source, out, out_t in ((w_mid, mid, mid_t), (w_last, last, last_t)):
        weights = source[...].astype(F32)
        for dx, dy, dz in OFFSETS:
            tap, at = dx * 9 + dy * 3 + dz, dy * 96 + dx * CH
            base[dz * CH : dz * CH + CH, at : at + CH] = weights[:, tap * CH : tap * CH + CH]
        spread(out)
        padded = jnp.concatenate([weights, jnp.zeros((CH, 80), F32)], 1)
        turned = jnp.concatenate([padded, jnp.zeros((112, 512), F32)], 0).T
        for dx, dy, dz in OFFSETS:
            tap, at = dx * 9 + dy * 3 + dz, (2 - dy) * 96 + (2 - dx) * CH
            to = (2 - dz) * CH
            base[to : to + CH, at : at + CH] = turned[tap * CH : tap * CH + CH, :CH]
        spread(out_t)
    base[...] = jnp.zeros_like(base)
    weights = w_first[...].astype(F32)
    for dx, dy, dz in OFFSETS:
        tap, at = dx * 9 + dy * 3 + dz, dx * 16 + dy
        base[dz * CH : dz * CH + CH, at : at + 1] = weights[:, tap : tap + 1]
    for dz in range(3):
        for x in range(BX + 2):
            at = (dz * (BX + 2) + x) * CH
            one[at : at + CH] = lane_roll(base[dz * CH : dz * CH + CH, :128], x * 16)
    head_f[...] = jnp.zeros_like(head_f)
    weights = w_head[...].astype(F32)
    for k in range(3):
        for x in range(BX):
            at = (k * BX + x) * BY
            for half in range(2):
                row = weights[k : k + 1, half * CH : half * CH + CH]
                to = half * 64 + x * CH
                head_f[at : at + BY, to : to + CH] = jnp.broadcast_to(row, (BY, CH))
    head_b[...] = head_f[...].T


def per_device(part_cells, part_offsets, part_counts, w_first, w_mid, w_last, w_head, cotangent):
    devices = part_counts.shape[1]
    vmem = pl.BlockSpec(memory_space=pltpu.VMEM)
    field = pltpu.VMEM((BY + 2, COLS, NZ), BF16)
    kept = pltpu.VMEM((BY, BX * CH, NZ), F32)
    table = pltpu.VMEM((192, 3 * COLS), BF16)
    hbm = pl.BlockSpec(memory_space=pltpu.HBM)
    slots = part_cells.shape[2]
    force, sums = pl.pallas_call(
        body,
        out_shape=(
            jax.ShapeDtypeStruct(cotangent.shape, BF16),
            jax.ShapeDtypeStruct((136, 128), F32),
        ),
        in_specs=[hbm, hbm, vmem, hbm, vmem, vmem, vmem, vmem],
        out_specs=[vmem] * 2,
        scratch_shapes=[
            pltpu.VMEM((devices, slots), jnp.int32),
            pltpu.VMEM((3, devices, slots), F32),
            pltpu.VMEM(cotangent.shape, BF16),
            pltpu.VMEM(cotangent.shape, BF16),
            pltpu.VMEM(cotangent.shape, BF16),
            pltpu.VMEM((devices * 8, 128), F32),
            pltpu.VMEM((devices * 8, 128), F32),
            pltpu.VMEM((2, NZ, 256 * GROUP), BF16),
            pltpu.VMEM((2, 192, 256 * GROUP), BF16),
            pltpu.VMEM((48, NZ), F32),
            pltpu.VMEM((5, 48, NZ), F32),
            pltpu.VMEM((128, NZ), F32),
            pltpu.VMEM((128, NZ), BF16),
            field, field, field, field, kept, kept,
            pltpu.VMEM((192, 384), F32),
            pltpu.VMEM((48, 384), F32),
            pltpu.VMEM((288, 128), F32),
            table, table, table, table,
            pltpu.VMEM((128, 128), F32),
            pltpu.VMEM((128, 128), F32),
            pltpu.VMEM((128, NZ), BF16),
            pltpu.VMEM((2, 64, 128), F32),
            pltpu.VMEM((2, 32, 128), F32),
            pltpu.VMEM((2, 3, 4, 32, 128), F32),
            pltpu.VMEM((8, 128), F32),
            pltpu.VMEM((8, 128), F32),
            pltpu.VMEM((devices // 2, 8, 128), F32),
            pltpu.SemaphoreType.DMA((3,)),
            pltpu.SemaphoreType.DMA((30,)),
            pltpu.SemaphoreType.DMA((30,)),
            pltpu.SemaphoreType.DMA((5,)),
            pltpu.SemaphoreType.DMA((5,)),
            pltpu.SemaphoreType.DMA((76,)),
            pltpu.SemaphoreType.DMA((76,)),
            pltpu.SemaphoreType.DMA((devices // (2 * GROUP),)),
            pltpu.SemaphoreType.DMA((devices // (2 * GROUP),)),
            pltpu.SemaphoreType.DMA((3,)),
            pltpu.SemaphoreType.DMA((3,)),
            pltpu.SemaphoreType.DMA((1,)),
            pltpu.SemaphoreType.DMA((1,)),
        ],
        compiler_params=pltpu.CompilerParams(
            collective_id=0, has_side_effects=True, vmem_limit_bytes=60 << 20
        ),
        name="level",
    )(part_cells, part_offsets.transpose(0, 2, 1, 3), part_counts, cotangent, w_first, w_mid, w_last, w_head)
    return pl.pallas_call(
        finish,
        out_shape=(
            jax.ShapeDtypeStruct(cotangent.shape, BF16),
            jax.ShapeDtypeStruct(w_first.shape, F32),
            jax.ShapeDtypeStruct(w_mid.shape, F32),
            jax.ShapeDtypeStruct(w_last.shape, F32),
            jax.ShapeDtypeStruct(w_head.shape, F32),
        ),
        in_specs=[vmem] * 2,
        out_specs=[vmem] * 5,
        compiler_params=pltpu.CompilerParams(vmem_limit_bytes=60 << 20),
        name="finish",
    )(force, sums)


def solution(mesh):
    in_specs = (
        P(("slab", "sub"), None, None),
        P(("slab", "sub"), None, None, None),
        P(("slab", "sub"), None),
        P(), P(), P(), P(),
        P(None, "slab", "sub", None),
    )
    out_specs = (P(None, "slab", "sub", None), P(), P(), P(), P())
    return jax.shard_map(
        per_device, mesh=mesh, in_specs=in_specs, out_specs=out_specs, check_vma=False
    )
```

```python
import functools
import math

import jax
import jax.numpy as jnp
from jax import lax
from jax.experimental import pallas as pl
from jax.experimental.pallas import tpu as pltpu
from jax.sharding import PartitionSpec as P

MESH = pl.DeviceIdType.MESH
F32 = jnp.float32
BF16 = jnp.bfloat16

BX, BY, NZ, CH = 4, 8, 256, 16
COLS = (BX + 2) * CH
CORE = slice(CH, CH + BX * CH)
GROUP = 4
X_ROW = (0, 8, 24, 32, 40)


def lane_roll(value, shift):
    return pltpu.roll(value, shift % value.shape[1], 1)


def dot(a, b):
    return jnp.dot(a, b, preferred_element_type=F32)


def dot_nt(a, b):
    return lax.dot_general(a, b, (((1,), (1,)), ((), ())), preferred_element_type=F32)


def join_z(stacked):
    rows = stacked.shape[0] // 3
    below = lane_roll(stacked[:rows], 1)
    above = lane_roll(stacked[2 * rows :], -1)
    return stacked[rows : 2 * rows] + below + above


def spread_z(grad):
    return jnp.concatenate([lane_roll(grad, -1), grad, lane_roll(grad, 1)], 0).astype(BF16)


def sigmoid(value):
    return 1.0 / (1.0 + jnp.exp(-value))


def slope(value):
    s = sigmoid(value)
    return s * (1.0 + value * (1.0 - s))


def source_terms(tile, half):
    cell = tile.astype(jnp.int32)
    where_z = jnp.where(cell < 0, -1, cell & 255).astype(F32)
    plane = lax.shift_right_arithmetic(cell, 8)

    def spread(value, row, rows=8):
        return jnp.broadcast_to(value[row : row + 1], (rows, 128))

    at = 4 * half
    z_at = spread(where_z, at + 3, NZ).astype(BF16)
    lanes_z = lax.broadcasted_iota(jnp.int32, (NZ, 128), 0).astype(F32).astype(BF16)
    hot = jnp.where(lanes_z == z_at, jnp.ones((), BF16), jnp.zeros((), BF16))
    plane = spread(plane, at + 3)
    at_x = lax.shift_right_arithmetic(plane, 3)
    at_y = plane & 7
    f = spread(tile, at)
    g = spread(tile, at + 1)
    h = spread(tile, at + 2)
    row = lax.broadcasted_iota(jnp.int32, (8, 128), 0)
    zero = jnp.zeros((8, 128), F32)
    weight_y = jnp.where(row == at_y, 1.0 - g, jnp.where(row == at_y + 1, g, zero))
    last_y = jnp.where(at_y == BY - 1, g, zero)
    weight_x = jnp.where(row == at_x, 1.0 - f, jnp.where(row == at_x + 1, f, zero))
    planes = []
    for i in range(BX + 1):
        here = jnp.where(at_x == i, 1.0 - f, jnp.where(at_x == i - 1, f, zero))
        planes.append(here * weight_y)
    planes.insert(2, weight_x * last_y)
    both = jnp.concatenate(planes, 0)
    tall = jnp.broadcast_to(h[:1], (48, 128))
    upper = both * tall
    lower = both - upper
    joint = jnp.concatenate([lower, upper], 0)
    high = joint.astype(BF16)
    low = (joint - high.astype(F32)).astype(BF16)
    return hot, jnp.concatenate([high, low], 0)


def body(
    cells_hbm, offsets_hbm, counts, ct_hbm, w_first, w_mid_in, w_last_in, w_head_in,
    force, sums,
    cells, offsets, ct_own, ct_in, force_s,
    packed, got, hot_s, wt_s, dep, dep_in, dens_f, dens, one, two, g_three, g_two, pre_one, pre_two, acc,
    base, w_one, w_mid, w_last, w_mid_t, w_last_t, head_f, head_b, ct_s,
    pay, half_in, ring, tile, tile_in, tiles,
    load, send, recv, send_d, recv_d, send_s, recv_s, send_p, recv_p, send_f, recv_f, send_m, recv_m,
):
    n_slab, n_sub = lax.axis_size("slab"), lax.axis_size("sub")
    slab, sub = lax.axis_index("slab"), lax.axis_index("sub")
    devices = n_slab * n_sub
    me = slab * n_sub + sub
    other = (sub + 1) % n_sub
    stop = ring_stop(slab)
    up, down = ring_slab((stop + 1) % n_slab), ring_slab((stop + n_slab - 1) % n_slab)
    neighbours = ((up, sub), (down, sub), (slab, other), (up, other), (down, other))
    worker, owner = (ring_slab(slab), other), (stop, other)
    axes = []
    for stride in (1, 4, 16):
        size = min(4, max(1, n_slab // stride))
        at = slab // stride % size
        axes.append((at, [slab + ((at + i) % size - at) * stride for i in range(1, size)]))

    loads = [
        pltpu.make_async_copy(src, dst, load.at[at])
        for at, (src, dst) in enumerate(
            ((cells_hbm.at[0], cells), (offsets_hbm.at[0], offsets), (ct_hbm, ct_own))
        )
    ]
    for copy in loads:
        copy.start()

    def partner(turn):
        to = (me + turn) % devices
        return (to // n_sub, to % n_sub), ring_stop(to // n_sub) * n_sub + (to + 1) % n_sub

    barrier = pltpu.get_barrier_semaphore()

    def greet(turn, carry):
        pl.semaphore_signal(barrier, inc=1, device_id=partner(turn)[0], device_id_type=MESH)
        return carry

    lax.fori_loop(1, devices, greet, 0)
    make_tables(w_first, w_mid_in, w_last_in, w_head_in, base, w_one, w_mid, w_last, w_mid_t,
                w_last_t, head_f, head_b)
    for copy in loads:
        copy.wait()

    diagonal = lax.broadcasted_iota(jnp.int32, (devices, devices), 0) == lax.broadcasted_iota(
        jnp.int32, (devices, devices), 1
    )
    used = jnp.broadcast_to(counts[...].astype(F32), (devices, devices))
    used = jnp.sum(jnp.where(diagonal, used, 0.0), 1, keepdims=True)
    slot = lax.broadcasted_iota(jnp.int32, (devices, 256), 1).astype(F32)
    live = jnp.where(slot < used, cells[...].astype(F32), -1.0)
    for first in range(0, devices, 8):
        some = slice(first, first + 8)
        for half in range(2):
            lanes = slice(half * 128, half * 128 + 128)
            for part in range(4):
                rows = pl.ds(first * 8 + 4 * half + part, 8, stride=8)
                packed[rows, :] = offsets[part, some, lanes] if part < 3 else live[some, lanes]

    def remote(src, dst, at, device, sends, recvs):
        return pltpu.make_async_remote_copy(
            src_ref=src, dst_ref=dst, send_sem=sends.at[at], recv_sem=recvs.at[at],
            device_id=device, device_id_type=MESH,
        )

    pl.semaphore_wait(barrier, devices - 1)

    def tile_rows(at):
        return pl.ds(pl.multiple_of(at * 8, 8), 8)

    def send_tile(turn, carry):
        device, brick = partner(turn)
        remote(
            packed.at[tile_rows(brick)], got.at[tile_rows(turn)], turn // (2 * GROUP), device,
            send_p, recv_p,
        ).start()
        return carry

    lax.fori_loop(1, devices, send_tile, 0)
    got[:8] = packed[tile_rows(partner(0)[1])]

    def arrived(step, tiles_in):
        rows = pl.ds(0, tiles_in * 8)
        return pltpu.make_async_copy(got.at[rows], got.at[rows], recv_p.at[step])

    def left(step, tiles_out):
        rows = pl.ds(0, tiles_out * 8)
        return pltpu.make_async_copy(packed.at[rows], packed.at[rows], send_p.at[step])

    def gather(step, total):
        for part in range(2):
            for k in range(GROUP):
                source = got[tile_rows(step * 2 * GROUP + part * GROUP + k)]
                for half in range(2):
                    hot, weights = source_terms(source, half)
                    at = k * 256 + half * 128
                    hot_s[part, :, at : at + 128] = hot
                    wt_s[part, :, at : at + 128] = weights
            result = dot_nt(wt_s[part], hot_s[part])
            total = total + result[:96] + result[96:]
        return total

    def wait_and_gather(step, total):
        arrived(step, 2 * GROUP).wait()
        return gather(step, total)

    arrived(0, 2 * GROUP - 1).wait()
    dep2 = gather(0, jnp.zeros((96, NZ), F32))
    dep2 = lax.fori_loop(1, devices // (2 * GROUP), wait_and_gather, dep2)
    dep[...] = dep2[:48] + lane_roll(dep2[48:], 1)

    upper_rows, lower_rows = pl.ds(16, 32), pl.ds(0, 24)
    copies = []
    for at, (device, rows) in enumerate(
        zip(neighbours, (upper_rows, lower_rows, pl.ds(0, 48), upper_rows, lower_rows))
    ):
        copies.append(remote(dep.at[rows], dep_in.at[at, rows], at, device, send_d, recv_d))
    for copy in copies:
        copy.start()

    dens_f[...] = jnp.zeros_like(dens_f)

    def place(source, source_x, x):
        base = (x + 2) * 16
        dens_f[base + 2 : base + 10] += source[X_ROW[source_x] : X_ROW[source_x] + 8]
        dens_f[base + 10 : base + 11] += source[16 + source_x : 17 + source_x]

    def place_other(source, source_x, x):
        base, row = (x + 2) * 16, X_ROW[source_x]
        dens_f[base : base + 2] += source[row + 6 : row + 8]
        dens_f[base + 2 : base + 3] += source[16 + source_x : 17 + source_x]
        dens_f[base + 10 : base + 12] += source[row : row + 2]

    ct_copy = remote(ct_own, ct_in, 0, worker, send_f, recv_f)
    ct_copy.start()
    for x in range(BX + 1):
        place(dep, x, x)
    left(0, 2 * GROUP - 1).wait()

    def sent(step, carry):
        left(step, 2 * GROUP).wait()
        return carry

    lax.fori_loop(1, devices // (2 * GROUP), sent, 0)
    for copy in copies:
        copy.wait()
    for x in (2, 3, 4):
        place(dep_in.at[0], x, x - 4)
    for x in (0, 1):
        place(dep_in.at[1], x, x + 4)
    for x in range(BX + 1):
        place_other(dep_in.at[2], x, x)
    for x in (2, 3, 4):
        place_other(dep_in.at[3], x, x - 4)
    for x in (0, 1):
        place_other(dep_in.at[4], x, x + 4)
    dens[...] = dens_f[...].astype(BF16)

    for y in range(BY + 2):
        taps = lane_roll(w_one[...], y).astype(BF16)
        pre = join_z(dot(taps, dens[...]))
        one[y] = (pre * sigmoid(pre)).astype(BF16)
        if 1 <= y <= BY:
            pre_one[y - 1] = pre[CORE]

    right, left_end = pl.ds(BX * CH, CH), pl.ds(CH, CH)
    before, after = pl.ds(0, CH), pl.ds((BX + 1) * CH, CH)
    core = pl.ds(CH, BX * CH)

    def rims(field, base, part):
        ys = pl.ds(1 + part * (BY // 2), BY // 2)
        edge, to = (1, BY + 1) if part == 0 else (BY, 0)
        plan = (
            ((slab, other), (edge, core), (to, core)),
            ((up, other), (edge, right), (to, before)),
            ((down, other), (edge, left_end), (to, after)),
            ((up, sub), (ys, right), (ys, before)),
            ((down, sub), (ys, left_end), (ys, after)),
        )
        started = []
        for at, (device, src, dst) in enumerate(plan):
            place = base + part * len(plan) + at
            copy = remote(field.at[src], field.at[dst], place, device, send, recv)
            copy.start()
            started.append(copy)
        return started

    def planes(field, y):
        return field[y : y + 3].reshape(3 * COLS, NZ)

    def conv(taps, field, y):
        return join_z(dot(taps[...], planes(field, y)))

    started = []
    for y in range(BY):
        pre = conv(w_mid, one, y)
        pre_two[y] = pre
        two[y + 1, CORE] = (pre * sigmoid(pre)).astype(BF16)
        if y % 4 == 3:
            started += rims(two, 0, y // 4)
    ct_copy.wait()
    ct_s[...] = jnp.zeros_like(ct_s)
    for k in range(3):
        for x in range(BX):
            at = (k * BX + x) * BY
            ct_s[at : at + BY] = ct_in[k, x]
    for copy in started:
        copy.wait()

    row_y = lax.broadcasted_iota(jnp.int32, (128, 128), 0) % BY
    lane_y = lax.broadcasted_iota(jnp.int32, (128, 128), 1) % BY
    out = jnp.zeros((96, NZ), F32)
    head = jnp.zeros((128, 128), F32)
    started = []
    for y in range(BY):
        pre = conv(w_last, two, y)
        s = sigmoid(pre)
        features = jnp.concatenate([(pre * s).astype(BF16), one[y + 1, CORE]], 0)
        taps = jnp.where(row_y == y, head_f[...], 0.0)[:96].astype(BF16)
        out = out + dot(taps, features)
        head = head + jnp.where(row_y == y, dot_nt(ct_s[...], features), 0.0)
        taps = jnp.where(lane_y == y, head_b[...], 0.0)[: BX * CH].astype(BF16)
        back = dot(taps, ct_s[...])
        g_three[y + 1, CORE] = (back * (s * (1.0 + pre * (1.0 - s)))).astype(BF16)
        if y % 4 == 3:
            started += rims(g_three, 10, y // 4)
    for k in range(3):
        for x in range(BX):
            at = (k * BX + x) * BY
            force_s[k, x] = out[at : at + BY].astype(BF16)
    force_copy = remote(force_s, force, 1, owner, send_f, recv_f)
    force_copy.start()

    def weight_grad(grads, field, out):
        acc[:, 3 * COLS :] = jnp.zeros((192, 96), F32)
        for y in range(BY):
            term = dot_nt(spread_z(grads[y + 1, CORE].astype(F32)), planes(field, y))
            if y == 0:
                acc[:, : 3 * COLS] = term
            else:
                acc[:, : 3 * COLS] += term
        rows = []
        for dz in range(3):
            total = jnp.zeros((CH, 384), F32)
            for x in range(BX):
                at = (dz * BX + x) * CH
                total = total + lane_roll(acc[at : at + CH], -CH * x)
            rows.append(total)
        joint = jnp.concatenate(rows, 0)
        lane = lax.broadcasted_iota(jnp.int32, joint.shape, 1)
        joint = jnp.where((lane % 96 < 48) & (lane < 3 * COLS), joint, 0.0)
        moved = [jnp.where(lane < 48, joint, 0.0)]
        for dy in (1, 2):
            inside = (lane >= 48 * dy) & (lane < 48 * dy + 48)
            moved.append(jnp.where(inside, lane_roll(joint, -48 * dy), 0.0))
        joint = moved[0] + moved[1] + moved[2]
        out[:48] = joint[:, :128]
        tail = joint[:CH, 128:256]
        for dz in (1, 2):
            tail = tail + lane_roll(joint[dz * CH : dz * CH + CH, 128:256], dz * CH)
        out[48:] = tail

    theirs = pl.ds(pl.multiple_of(other * 32, 8), 32)
    mine = pl.ds(pl.multiple_of(sub * 32, 8), 32)

    class Sum:
        def __init__(self, at):
            self.at, self.next, self.copies = at, at * 38, []

        def begin(self, src, dst, device):
            self.copies.append(remote(src, dst, self.next, device, send_s, recv_s))
            self.copies[-1].start()
            self.next += 1

        def end(self):
            for copy in self.copies:
                copy.wait()
            self.copies = []

        def across(self):
            self.begin(pay.at[self.at, theirs], half_in.at[self.at], (slab, other))

        def joined(self):
            self.end()
            return pay[self.at, mine] + half_in[self.at]

        def out(self, turn, total):
            for part in range(4):
                at, peers = axes[(part + turn) % 3]
                rows = pl.ds(part * 8, 8)
                ring[self.at, turn, at, rows] = total[part * 8 : part * 8 + 8]
                for peer in peers:
                    slot = ring.at[self.at, turn, at, rows]
                    self.begin(slot, slot, (peer, sub))

        def back(self, turn):
            self.end()
            parts = []
            for part in range(4):
                rows = slice(part * 8, part * 8 + 8)
                value = ring[self.at, turn, 0, rows]
                for slot in range(1, len(axes[(part + turn) % 3][1]) + 1):
                    value = value + ring[self.at, turn, slot, rows]
                parts.append(value)
            return jnp.concatenate(parts, 0)

        def share(self, total):
            rows = pl.ds(pl.multiple_of(self.at * 64 + sub * 32, 8), 32)
            sums[rows] = total * scale
            self.begin(sums.at[rows], sums.at[rows], (slab, other))

    scale = 1.0 / math.sqrt(BX * n_slab * BY * n_sub * NZ)
    sum_last, sum_mid = Sum(0), Sum(1)

    weight_grad(g_three, two, pay.at[0])
    row = lax.broadcasted_iota(jnp.int32, (128, 128), 0)
    lane = lax.broadcasted_iota(jnp.int32, (128, 128), 1)
    head = jnp.where(lane % 64 // CH == row // BY % BX, head, 0.0)
    kept = jnp.concatenate(
        [jnp.sum(head[k * 32 : k * 32 + 32], 0, keepdims=True) for k in range(3)]
        + [jnp.zeros((5, 128), F32)],
        0,
    )
    kept = kept + lane_roll(kept, -2 * CH)
    kept = kept + lane_roll(kept, -CH)
    lane = lax.broadcasted_iota(jnp.int32, (8, 128), 1)
    top = jnp.where(lane < CH, kept, 0.0) + jnp.where(
        (lane >= CH) & (lane < 2 * CH), lane_roll(kept, -48), 0.0
    )
    pay[0, 48:56] += lane_roll(top, 48)
    sum_last.across()
    for copy in started:
        copy.wait()

    started = []
    for y in range(BY):
        back = conv(w_last_t, g_three, y)
        g_two[y + 1, CORE] = (back * slope(pre_two[y])).astype(BF16)
        if y % 4 == 3:
            started += rims(g_two, 20, y // 4)
    sum_last.out(0, sum_last.joined())
    weight_grad(g_two, one, pay.at[1])
    sum_mid.across()
    sum_last.out(1, sum_last.back(0))
    for copy in started:
        copy.wait()
    sum_mid.out(0, sum_mid.joined())

    first = jnp.zeros((192, 128), F32)
    for y in range(BY):
        taps = jnp.where(lane_y == y, head_b[...], 0.0)[BX * CH :].astype(BF16)
        back = conv(w_mid_t, g_two, y) + dot(taps, ct_s[...])
        grad = (back * slope(pre_one[y])).astype(BF16).astype(F32)
        first = first + lane_roll(dot_nt(spread_z(grad), dens[...]), -y)
    rows = []
    for dz in range(3):
        total = jnp.zeros((CH, 128), F32)
        for x in range(BX):
            at = (dz * BX + x) * CH
            total = total + lane_roll(first[at : at + CH], -(16 * x + 17))
        rows.append(total)
    joint = jnp.concatenate(rows, 0)
    lane = lax.broadcasted_iota(jnp.int32, joint.shape, 1)
    joint = jnp.where((lane % 16 < 3) & (lane < 48), joint, 0.0)
    value = jnp.zeros((8, 128), F32)
    for block, shift in enumerate(BLOCK_LANE):
        value = value + lane_roll(joint[block * 8 : block * 8 + 8], shift)
    tile[...] = value
    tile_copy = remote(tile, tile_in, 2, (slab, other), send_f, recv_f)
    tile_copy.start()
    sum_mid.out(1, sum_mid.back(0))
    sum_last.out(2, sum_last.back(1))
    tile_copy.wait()
    tiles[slab] = tile[...] + tile_in[...]
    if n_slab > 1:

        def spread_tile(turn, carry):
            peer = (slab + 1 + (turn + n_slab * 2 // 3) % (n_slab - 1)) % n_slab
            remote(tiles.at[slab], tiles.at[slab], 0, (peer, sub), send_m, recv_m).start()
            return carry

        lax.fori_loop(0, n_slab - 1, spread_tile, 0)
    sum_mid.out(2, sum_mid.back(1))
    sum_last.share(sum_last.back(2))
    sum_mid.share(sum_mid.back(2))
    if n_slab > 1:
        some = pl.ds(0, n_slab - 1)
        pltpu.make_async_copy(tiles.at[some], tiles.at[some], recv_m.at[0]).wait()
        pltpu.make_async_copy(tiles.at[some], tiles.at[some], send_m.at[0]).wait()
    sums[128:136] = jnp.sum(tiles[...], 0) * scale
    sum_last.end()
    sum_mid.end()
    force_copy.wait()


def ring_stop(slab):
    y = (slab // 4 + slab // 16) % 4
    return slab // 16 * 16 + y * 4 + (slab + y) % 4


def ring_slab(stop):
    z, y = stop // 16, stop // 4 % 4
    return z * 16 + (y + 4 - z) % 4 * 4 + (stop + 4 - y) % 4


def finish(force_in, sums, force, grad_first, grad_mid, grad_last, grad_head):
    force[...] = force_in[...]
    for dx, dy, dz in OFFSETS:
        tap, rows, at = dx * 9 + dy * 3 + dz, dz * CH, dy * 48 + dx * CH
        if at == 128:
            rows, at = 48, dz * CH
        for first, out in ((64, grad_mid), (0, grad_last)):
            block = sums[first + rows : first + rows + CH, at : at + CH]
            out[:, tap * CH : tap * CH + CH] = block
        for half in range(2):
            at = BLOCK_LANE[2 * dz + half] + dx * CH + dy
            grad_first[half * 8 : half * 8 + 8, tap : tap + 1] = sums[128:136, at : at + 1]
    grad_head[...] = sums[48:51, 48:80]


BLOCK_LANE = (0, 3, 6, 9, 12, 48)
OFFSETS = [(dx, dy, dz) for dx in range(3) for dy in range(3) for dz in range(3)]


def make_tables(w_first, w_mid, w_last, w_head, base, one, mid, last, mid_t, last_t, head_f, head_b):
    def spread(out):
        for dz in range(3):
            for x in range(BX):
                at = (dz * BX + x) * CH
                moved = lane_roll(base[dz * CH : dz * CH + CH], x * CH)
                out[at : at + CH] = moved[:, : 3 * COLS].astype(BF16)

    base[...] = jnp.zeros_like(base)
    for source, out, out_t in ((w_mid, mid, mid_t), (w_last, last, last_t)):
        weights = source[...].astype(F32)
        for dx, dy, dz in OFFSETS:
            tap, at = dx * 9 + dy * 3 + dz, dy * 96 + dx * CH
            base[dz * CH : dz * CH + CH, at : at + CH] = weights[:, tap * CH : tap * CH + CH]
        spread(out)
        padded = jnp.concatenate([weights, jnp.zeros((CH, 80), F32)], 1)
        turned = jnp.concatenate([padded, jnp.zeros((112, 512), F32)], 0).T
        for dx, dy, dz in OFFSETS:
            tap, at = dx * 9 + dy * 3 + dz, (2 - dy) * 96 + (2 - dx) * CH
            to = (2 - dz) * CH
            base[to : to + CH, at : at + CH] = turned[tap * CH : tap * CH + CH, :CH]
        spread(out_t)
    base[...] = jnp.zeros_like(base)
    weights = w_first[...].astype(F32)
    for dx, dy, dz in OFFSETS:
        tap, at = dx * 9 + dy * 3 + dz, dx * 16 + dy
        base[dz * CH : dz * CH + CH, at : at + 1] = weights[:, tap : tap + 1]
    for dz in range(3):
        for x in range(BX + 2):
            at = (dz * (BX + 2) + x) * CH
            one[at : at + CH] = lane_roll(base[dz * CH : dz * CH + CH, :128], x * 16)
    head_f[...] = jnp.zeros_like(head_f)
    weights = w_head[...].astype(F32)
    for k in range(3):
        for x in range(BX):
            at = (k * BX + x) * BY
            for half in range(2):
                row = weights[k : k + 1, half * CH : half * CH + CH]
                to = half * 64 + x * CH
                head_f[at : at + BY, to : to + CH] = jnp.broadcast_to(row, (BY, CH))
    head_b[...] = head_f[...].T


def per_device(part_cells, part_offsets, part_counts, w_first, w_mid, w_last, w_head, cotangent):
    devices = part_counts.shape[1]
    vmem = pl.BlockSpec(memory_space=pltpu.VMEM)
    field = pltpu.VMEM((BY + 2, COLS, NZ), BF16)
    kept = pltpu.VMEM((BY, BX * CH, NZ), F32)
    table = pltpu.VMEM((192, 3 * COLS), BF16)
    hbm = pl.BlockSpec(memory_space=pltpu.HBM)
    slots = part_cells.shape[2]
    force, sums = pl.pallas_call(
        body,
        out_shape=(
            jax.ShapeDtypeStruct(cotangent.shape, BF16),
            jax.ShapeDtypeStruct((136, 128), F32),
        ),
        in_specs=[hbm, hbm, vmem, hbm, vmem, vmem, vmem, vmem],
        out_specs=[vmem] * 2,
        scratch_shapes=[
            pltpu.VMEM((devices, slots), jnp.int32),
            pltpu.VMEM((3, devices, slots), F32),
            pltpu.VMEM(cotangent.shape, BF16),
            pltpu.VMEM(cotangent.shape, BF16),
            pltpu.VMEM(cotangent.shape, BF16),
            pltpu.VMEM((devices * 8, 128), F32),
            pltpu.VMEM((devices * 8, 128), F32),
            pltpu.VMEM((2, NZ, 256 * GROUP), BF16),
            pltpu.VMEM((2, 192, 256 * GROUP), BF16),
            pltpu.VMEM((48, NZ), F32),
            pltpu.VMEM((5, 48, NZ), F32),
            pltpu.VMEM((128, NZ), F32),
            pltpu.VMEM((128, NZ), BF16),
            field, field, field, field, kept, kept,
            pltpu.VMEM((192, 384), F32),
            pltpu.VMEM((48, 384), F32),
            pltpu.VMEM((288, 128), F32),
            table, table, table, table,
            pltpu.VMEM((128, 128), F32),
            pltpu.VMEM((128, 128), F32),
            pltpu.VMEM((128, NZ), BF16),
            pltpu.VMEM((2, 64, 128), F32),
            pltpu.VMEM((2, 32, 128), F32),
            pltpu.VMEM((2, 3, 4, 32, 128), F32),
            pltpu.VMEM((8, 128), F32),
            pltpu.VMEM((8, 128), F32),
            pltpu.VMEM((devices // 2, 8, 128), F32),
            pltpu.SemaphoreType.DMA((3,)),
            pltpu.SemaphoreType.DMA((30,)),
            pltpu.SemaphoreType.DMA((30,)),
            pltpu.SemaphoreType.DMA((5,)),
            pltpu.SemaphoreType.DMA((5,)),
            pltpu.SemaphoreType.DMA((76,)),
            pltpu.SemaphoreType.DMA((76,)),
            pltpu.SemaphoreType.DMA((devices // (2 * GROUP),)),
            pltpu.SemaphoreType.DMA((devices // (2 * GROUP),)),
            pltpu.SemaphoreType.DMA((3,)),
            pltpu.SemaphoreType.DMA((3,)),
            pltpu.SemaphoreType.DMA((1,)),
            pltpu.SemaphoreType.DMA((1,)),
        ],
        compiler_params=pltpu.CompilerParams(
            collective_id=0, has_side_effects=True, vmem_limit_bytes=60 << 20
        ),
        name="level",
    )(part_cells, part_offsets.transpose(0, 2, 1, 3), part_counts, cotangent, w_first, w_mid, w_last, w_head)
    return pl.pallas_call(
        finish,
        out_shape=(
            jax.ShapeDtypeStruct(cotangent.shape, BF16),
            jax.ShapeDtypeStruct(w_first.shape, F32),
            jax.ShapeDtypeStruct(w_mid.shape, F32),
            jax.ShapeDtypeStruct(w_last.shape, F32),
            jax.ShapeDtypeStruct(w_head.shape, F32),
        ),
        in_specs=[vmem] * 2,
        out_specs=[vmem] * 5,
        compiler_params=pltpu.CompilerParams(vmem_limit_bytes=60 << 20),
        name="finish",
    )(force, sums)


def solution(mesh):
    in_specs = (
        P(("slab", "sub"), None, None),
        P(("slab", "sub"), None, None, None),
        P(("slab", "sub"), None),
        P(), P(), P(), P(),
        P(None, "slab", "sub", None),
    )
    out_specs = (P(None, "slab", "sub", None), P(), P(), P(), P())
    return jax.shard_map(
        per_device, mesh=mesh, in_specs=in_specs, out_specs=out_specs, check_vma=False
    )
```
